256 devices in a mesh: vec: 16 (over z_hi, x, core), dom: 16 (over y, z_lo).
Axes of the slice: x: 4, y: 4, z: 8 (z_hi: 2, z_lo: 4; z = z_hi * 4 + z_lo), core: 2. Of those that a mesh axis runs over, the one named last changes fastest.
Arguments:
- vectors: float32 [512, 128, 32, 128], P('vec', 'dom'), may hold values from -6 to 6
- coefficient: float32 [128, 32, 128], P('dom', 'vec'), may hold values from 0.25 to 2.5
- ritz: bfloat16 [128, 32, 128, 1024], P('dom', 'vec'), may hold values from -0.0390625 to 0.0390625
Outputs:
- residual: float32 [512, 128, 32, 128], P(None, 'dom', 'vec')
The draws below stay inside these ranges and needn't reach their ends.
All inputs are finite; a program needn't handle non-finite values.
Results may differ from the reference program's by a relative error of at most 0.003.
Values may be sent and summed in bfloat16 or wider, within the bound.
No kernel may reach another device: no remote copies, remote signals or barrier semaphores. Data moves between devices by JAX's collectives and lax.ppermute only.
A program may use at most 128 MiB of HBM per device.

```python
import math
import jax
import jax.numpy as jnp
from jax import lax

VEC_DEV = 32
NY = 32
NX = 128
K = 1024
SWEEPS = 4
V = 512
NZ = 128


def level_of(rng, dims, split, least, high):
    def one(dim, blocks):
        steps = jax.random.uniform(jax.random.fold_in(jax.random.fold_in(rng, 6), dim), (blocks,), jnp.float32, least / len(split), high / len(split))
        return jnp.repeat(jnp.exp(steps), dims[dim] // blocks).reshape((-1,) + (1,) * (len(dims) - dim - 1))

    gain = one(*split[0])
    for cut in split[1:]:
        gain = gain * one(*cut)
    return gain


def bell_draw(own_key, shape, scale, limit, cuts=(), kind=jnp.bfloat16):
    result = scale * jax.random.normal(own_key, shape, jnp.float32)
    if cuts:
        result = result * level_of(own_key, shape, cuts, -0.22, 0.18)
    return jnp.clip(result, -limit, limit).astype(kind)


def setup_inputs(seed: int = 0) -> dict:
    seeds = jax.random.split(jax.random.key(seed), 4)
    return {
        "vectors": bell_draw(seeds[0], (V, NZ, NY, NX), 1.0, 6.0, ((0, 16), (1, 16)), jnp.float32),
        "coefficient": jnp.clip(jnp.exp(math.log(2.5) - 2.3025851 * jax.random.uniform(seeds[1], (NZ, NY, NX), jnp.float32) ** level_of(seeds[1], (NZ, NY, NX), ((0, 16), (1, 16)), -0.2, 0.2)), 0.25, 2.5),
        "ritz": bell_draw(seeds[2], (NZ, NY, NX, K), ((K * NX * NY * NZ) ** 0.5) ** -0.5, 0.0390625, ((0, 16), (1, 16))),
    }


center_value = 7.125
half_range = 7.0


def scaled(field, coefficient):
    padded = jnp.pad(field, ((0, 0), (1, 1), (1, 1), (1, 1)))
    beside = padded[:, 2:, 1:-1, 1:-1] + padded[:, :-2, 1:-1, 1:-1]
    beside = beside + padded[:, 1:-1, 2:, 1:-1] + padded[:, 1:-1, :-2, 1:-1]
    beside = beside + padded[:, 1:-1, 1:-1, 2:] + padded[:, 1:-1, 1:-1, :-2]
    return ((6.0 + coefficient - center_value) * field - beside) / half_range


def filter_block(block, coefficient):
    previous = block
    current = scaled(block, coefficient)
    for sweep in range(SWEEPS - 1):
        previous, current = current, 2.0 * scaled(current, coefficient) - previous
    return current


def reference(vectors, coefficient, ritz):
    blocks = vectors.reshape(V // VEC_DEV, VEC_DEV, NZ, NY, NX)
    filtered = lax.map(lambda block: filter_block(block, coefficient), blocks).reshape(V, NZ * NY * NX)
    ritz_matrix = ritz.reshape(NZ * NY * NX, K)
    coeffs = jnp.dot(filtered.astype(jnp.bfloat16), ritz_matrix, preferred_element_type=jnp.float32)
    removed = lax.dot_general(coeffs.astype(jnp.bfloat16), ritz_matrix, (((1,), (1,)), ((), ())), preferred_element_type=jnp.float32)
    return (filtered - removed).reshape(V, NZ, NY, NX)
```

```python
import functools

import jax
import jax.numpy as jnp
from jax import lax
from jax.experimental import pallas as pl
from jax.experimental.pallas import tpu as pltpu
from jax.sharding import Mesh, PartitionSpec as P

bf16 = jnp.bfloat16
f32 = jnp.float32

VEC = ("zh", "x", "c")
DOM = ("y", "zl")
NEAR = ("x", "c", "y")
LINE = ("zh", "zl")
HALO = 4
GROUP = 16


def filter_kernel(ends_ref, own_ref, low_ref, high_ref, diag_ref, out_ref, even, odd):
    planes, rows = own_ref.shape[0], own_ref.shape[1]
    total = planes + 2 * HALO
    lanes = own_ref.shape[3]
    lane = lax.broadcasted_iota(jnp.int32, (GROUP, lanes), 1)
    first, last = lane == 0, lane == lanes - 1

    def fill(p, carry):
        for y in range(rows):
            even[p, y] = low_ref[p, y].astype(f32)
            even[p + HALO + planes, y] = high_ref[p, y].astype(f32)
        return carry

    lax.fori_loop(0, HALO, fill, 0)

    def copy(p, carry):
        for y in range(rows):
            even[p + HALO, y] = own_ref[p, y]
        return carry

    lax.fori_loop(0, planes, copy, 0)

    def step(source, target, weight, reach, scale):
        def plane(p, carry):
            below = None
            here = source[p, 0]
            for y in range(rows):
                above = source[p, y + 1] if y + 1 < rows else None
                left = jnp.where(first, 0.0, pltpu.roll(here, 1, 1))
                right = jnp.where(last, 0.0, pltpu.roll(here, lanes - 1, 1))
                beside = (source[p - 1, y] + source[p + 1, y]) + (left + right)
                if below is not None:
                    beside = beside + below
                if above is not None:
                    beside = beside + above
                value = diag_ref[p, pl.ds(y, 1), :] * here - beside
                if weight:
                    value = value - weight * target[p, y]
                if scale:
                    out_ref[y // 2, 2 * (p - HALO) + y % 2] = (value * scale).astype(bf16)
                else:
                    target[p, y] = value
                below, here = here, above
            return carry

        lax.fori_loop(reach, total - reach, plane, 0)
        if reach < HALO:
            zero = jnp.zeros((GROUP, lanes), f32)

            def clear(at):
                def one(p, carry):
                    for y in range(rows):
                        target[at + p, y] = zero
                    return carry

                lax.fori_loop(0, HALO - reach, one, 0)

            @pl.when(ends_ref[0] == 1)
            def _():
                clear(reach)

            @pl.when(ends_ref[1] == 1)
            def _():
                clear(HALO + planes)

    step(even, odd, 0.0, 1, 0.0)
    step(odd, even, 24.5, 2, 0.0)
    step(even, odd, 12.25, 3, 0.0)
    step(odd, even, 12.25, 4, 8.0 / 2401.0)


def filtered(ends, own, low, high, diag):
    planes, rows, vectors, lanes = own.shape
    total = planes + 2 * HALO
    return pl.pallas_call(
        filter_kernel,
        out_shape=jax.ShapeDtypeStruct((rows // 2, 2 * planes, vectors, lanes), bf16),
        grid=(vectors // GROUP,),
        in_specs=[
            pl.BlockSpec(memory_space=pltpu.SMEM),
            pl.BlockSpec((planes, rows, GROUP, lanes), lambda g: (0, 0, g, 0)),
            pl.BlockSpec((HALO, rows, GROUP, lanes), lambda g: (0, 0, g, 0)),
            pl.BlockSpec((HALO, rows, GROUP, lanes), lambda g: (0, 0, g, 0)),
            pl.BlockSpec((total, rows, lanes), lambda g: (0, 0, 0)),
        ],
        out_specs=pl.BlockSpec((rows // 2, 2 * planes, GROUP, lanes), lambda g: (0, 0, g, 0)),
        scratch_shapes=[pltpu.VMEM((total, rows, GROUP, lanes), f32)] * 2,
        compiler_params=pltpu.CompilerParams(vmem_limit_bytes=48 << 20),
        cost_estimate=pl.CostEstimate(
            flops=12 * 44 * rows * vectors * lanes, bytes_accessed=10 << 20, transcendentals=0
        ),
    )(ends, own, low, high, diag)


def project_kernel(cells_ref, ritz_ref, out_ref, total):
    step = pl.program_id(0)
    blocks, _, vectors, lanes = cells_ref.shape

    @pl.when(step == 0)
    def _():
        total[...] = jnp.zeros_like(total)

    pair = jnp.concatenate(
        [cells_ref[:, 0].reshape(-1, lanes), cells_ref[:, 1].reshape(-1, lanes)], axis=1
    )
    total[...] += jnp.dot(
        pair, ritz_ref[...].reshape(2 * lanes, -1), preferred_element_type=f32
    )

    @pl.when(step == pl.num_programs(0) - 1)
    def _():
        out_ref[...] = total[...].astype(out_ref.dtype)


def projected(cells, ritz):
    blocks, rows, vectors, lanes = cells.shape
    kept = ritz.shape[2]
    count = blocks * vectors
    return pl.pallas_call(
        project_kernel,
        out_shape=jax.ShapeDtypeStruct((count, kept), bf16),
        grid=(rows // 2,),
        in_specs=[
            pl.BlockSpec((blocks, 2, vectors, lanes), lambda r: (0, r, 0, 0)),
            pl.BlockSpec((2, lanes, kept), lambda r: (r, 0, 0)),
        ],
        out_specs=pl.BlockSpec((count, kept), lambda r: (0, 0)),
        scratch_shapes=[pltpu.VMEM((count, kept), f32)],
        cost_estimate=pl.CostEstimate(
            flops=2 * count * rows * lanes * kept, bytes_accessed=7 << 20, transcendentals=0
        ),
    )(cells, ritz)


def remove_kernel(coeffs_ref, ritz_ref, cells_ref, out_ref):
    rows, lanes = cells_ref.shape[1], cells_ref.shape[3]
    count = coeffs_ref.shape[0]
    for r in range(0, rows, 2):
        removed = lax.dot_general(
            coeffs_ref[...],
            ritz_ref[r : r + 2].reshape(2 * lanes, -1),
            (((1,), (1,)), ((), ())),
            preferred_element_type=f32,
        )
        for k in range(2):
            held = cells_ref[:, r + k].reshape(count, lanes).astype(f32)
            out_ref[pl.ds(r + k, count, stride=rows), :] = (
                held - removed[:, k * lanes : (k + 1) * lanes]
            )


def residual(coeffs, ritz, cells, parts):
    blocks, rows, vectors, lanes = cells.shape
    kept = ritz.shape[2]
    count = blocks * vectors
    return pl.pallas_call(
        remove_kernel,
        out_shape=jax.ShapeDtypeStruct((count * rows, lanes), f32),
        grid=(parts,),
        in_specs=[
            pl.BlockSpec((count // parts, kept), lambda g: (g, 0)),
            pl.BlockSpec((rows, lanes, kept), lambda g: (0, 0, 0)),
            pl.BlockSpec((blocks // parts, rows, vectors, lanes), lambda g: (g, 0, 0, 0)),
        ],
        out_specs=pl.BlockSpec((count // parts * rows, lanes), lambda g: (g, 0)),
        cost_estimate=pl.CostEstimate(
            flops=2 * count * rows * lanes * kept, bytes_accessed=11 << 20, transcendentals=0
        ),
    )(coeffs, ritz, cells)


def summed(partial):
    near = lax.axis_size(NEAR)
    line = lax.axis_size(LINE)
    count, kept = partial.shape
    blocks = lax.all_to_all(
        partial.reshape(near, count // near, kept), NEAR, 0, 0, tiled=True
    )
    blocks = jnp.sum(blocks.astype(f32), axis=0).reshape(line, -1, kept)
    blocks = jnp.sum(lax.all_to_all(blocks, LINE, 0, 0, tiled=True), axis=0).astype(bf16)
    blocks = from_everyone(blocks, LINE).reshape(-1, kept)
    return from_everyone(blocks, NEAR).reshape(count, kept)


def from_everyone(value, axis):
    copies = jnp.broadcast_to(value, (lax.axis_size(axis), *value.shape))
    return lax.all_to_all(copies, axis, split_axis=0, concat_axis=0, tiled=True)


def swap_ends(low, high):
    count = lax.axis_size(DOM)
    from_below = lax.ppermute(high, DOM, [(i, i + 1) for i in range(count - 1)])
    from_above = lax.ppermute(low, DOM, [(i + 1, i) for i in range(count - 1)])
    return from_below, from_above


def body(vectors, coefficient, ritz):
    own = vectors.transpose(1, 2, 0, 3)
    low, high = swap_ends(own[:HALO].astype(bf16), own[-HALO:].astype(bf16))
    below, above = swap_ends(coefficient[:HALO], coefficient[-HALO:])
    diag = jnp.concatenate([below, coefficient, above], axis=0)
    diag = from_everyone(diag, VEC).transpose(1, 0, 2, 3)
    diag = diag.reshape(diag.shape[0], -1, diag.shape[3]) + (6.0 - 7.125)
    place = lax.axis_index(DOM)
    ends = jnp.stack([place == 0, place == lax.axis_size(DOM) - 1]).astype(jnp.int32)
    blocks = filtered(ends, own, low, high, diag)
    cells = lax.all_to_all(blocks, VEC, 0, 0, tiled=True)
    ritz_rows = ritz.reshape(-1, *ritz.shape[2:])
    coeffs = summed(projected(cells, ritz_rows))
    out = residual(coeffs, ritz_rows, cells, 2)
    return out.reshape(-1, *coefficient.shape)


def solution(mesh):
    fine = Mesh(mesh.devices.reshape(2, 4, 2, 4, 4), ("zh", "x", "c", "y", "zl"))
    placed = (P(VEC, DOM, None, None), P(DOM, VEC, None), P(DOM, VEC, None, None))
    return jax.shard_map(
        body, mesh=fine, in_specs=placed, out_specs=P(None, DOM, VEC, None), check_vma=False
    )
```

```python
import functools

import jax
import jax.numpy as jnp
from jax import lax
from jax.experimental import pallas as pl
from jax.experimental.pallas import tpu as pltpu
from jax.sharding import Mesh, PartitionSpec as P

bf16 = jnp.bfloat16
f32 = jnp.float32

VEC = ("zh", "x", "c")
DOM = ("y", "zl")
NEAR = ("x", "c", "y")
LINE = ("zh", "zl")
HALO = 4
GROUP = 16
CHUNKS = 2
PARTS = 2


def spread_kernel(first_ref, second_ref, *out_refs):
    for source, low, own in ((first_ref, *out_refs[:2]), (second_ref, *out_refs[2:])):
        vectors, rows, lanes = source.shape
        flat = source.reshape(vectors * rows, lanes)
        for y in range(rows):
            value = flat[pl.ds(y, vectors, stride=rows), :]
            low[0, y] = value.astype(bf16)
            own[0, y] = value


def spread(cells, rows, chunk, size):
    planes, lanes = cells.shape[1] // rows, cells.shape[2]
    half = planes // 2
    shape = (half, rows, size, lanes)
    out = pl.BlockSpec((1, rows, size, lanes), lambda p: (p, 0, 0, 0))
    return pl.pallas_call(
        spread_kernel,
        out_shape=[jax.ShapeDtypeStruct(shape, bf16), jax.ShapeDtypeStruct(shape, f32)] * 2,
        grid=(half,),
        in_specs=[
            pl.BlockSpec((size, rows, lanes), lambda p: (chunk, p, 0)),
            pl.BlockSpec((size, rows, lanes), lambda p: (chunk, p + half, 0)),
        ],
        out_specs=[out] * 4,
        cost_estimate=pl.CostEstimate(
            flops=size * planes * rows * lanes,
            bytes_accessed=10 * size * planes * rows * lanes,
            transcendentals=0,
        ),
    )(cells, cells)


def filter_kernel(ends_ref, near_ref, far_ref, low_ref, high_ref, diag_ref, out_ref, even, odd):
    half, rows, lanes = near_ref.shape[0], near_ref.shape[1], near_ref.shape[3]
    planes = 2 * half
    total = planes + 2 * HALO
    lane = lax.broadcasted_iota(jnp.int32, (GROUP, lanes), 1)
    first, last = lane == 0, lane == lanes - 1

    def fill(p, carry):
        for y in range(rows):
            even[p, y] = low_ref[p, y].astype(f32)
            even[p + HALO + planes, y] = high_ref[p, y].astype(f32)
        return carry

    lax.fori_loop(0, HALO, fill, 0)

    def copy(p, carry):
        for y in range(rows):
            even[p + HALO, y] = near_ref[p, y]
            even[p + HALO + half, y] = far_ref[p, y]
        return carry

    lax.fori_loop(0, half, copy, 0)

    def step(source, target, weight, reach, scale):
        def plane(p, carry):
            below = None
            here = source[p, 0]
            for y in range(rows):
                above = source[p, y + 1] if y + 1 < rows else None
                left = jnp.where(first, 0.0, pltpu.roll(here, 1, 1))
                right = jnp.where(last, 0.0, pltpu.roll(here, lanes - 1, 1))
                beside = (source[p - 1, y] + source[p + 1, y]) + (left + right)
                if below is not None:
                    beside = beside + below
                if above is not None:
                    beside = beside + above
                value = diag_ref[p, pl.ds(y, 1), :] * here - beside
                if weight:
                    value = value - weight * target[p, y]
                if scale:
                    out_ref[y // 2, 2 * (p - HALO) + y % 2] = (value * scale).astype(bf16)
                else:
                    target[p, y] = value
                below, here = here, above
            return carry

        lax.fori_loop(reach, total - reach, plane, 0)
        if reach < HALO:
            zero = jnp.zeros((GROUP, lanes), f32)

            def clear(at):
                def one(p, carry):
                    for y in range(rows):
                        target[at + p, y] = zero
                    return carry

                lax.fori_loop(0, HALO - reach, one, 0)

            @pl.when(ends_ref[0] == 1)
            def _():
                clear(reach)

            @pl.when(ends_ref[1] == 1)
            def _():
                clear(HALO + planes)

    step(even, odd, 0.0, 1, 0.0)
    step(odd, even, 24.5, 2, 0.0)
    step(even, odd, 12.25, 3, 0.0)
    step(odd, even, 12.25, 4, 8.0 / 2401.0)


def filtered(ends, near, far, low, high, diag):
    half, rows, vectors, lanes = near.shape
    planes = 2 * half
    total = planes + 2 * HALO
    return pl.pallas_call(
        filter_kernel,
        out_shape=jax.ShapeDtypeStruct((rows // 2, 2 * planes, vectors, lanes), bf16),
        grid=(vectors // GROUP,),
        in_specs=[
            pl.BlockSpec(memory_space=pltpu.SMEM),
            pl.BlockSpec((half, rows, GROUP, lanes), lambda g: (0, 0, g, 0)),
            pl.BlockSpec((half, rows, GROUP, lanes), lambda g: (0, 0, g, 0)),
            pl.BlockSpec((HALO, rows, GROUP, lanes), lambda g: (0, 0, g, 0)),
            pl.BlockSpec((HALO, rows, GROUP, lanes), lambda g: (0, 0, g, 0)),
            pl.BlockSpec((total, rows, lanes), lambda g: (0, 0, 0)),
        ],
        out_specs=pl.BlockSpec((rows // 2, 2 * planes, GROUP, lanes), lambda g: (0, 0, g, 0)),
        scratch_shapes=[pltpu.VMEM((total, rows, GROUP, lanes), f32)] * 2,
        compiler_params=pltpu.CompilerParams(vmem_limit_bytes=24 << 20),
        cost_estimate=pl.CostEstimate(
            flops=12 * 44 * rows * vectors * lanes, bytes_accessed=10 << 20, transcendentals=0
        ),
    )(ends, near, far, low, high, diag)


def project_kernel(cells_ref, ritz_ref, *refs):
    out_ref, total = refs[-2:]
    step = pl.program_id(0)
    lanes = cells_ref.shape[3]

    @pl.when(step == 0)
    def _():
        total[...] = jnp.zeros_like(total)

    pair = jnp.concatenate(
        [cells_ref[:, 0].reshape(-1, lanes), cells_ref[:, 1].reshape(-1, lanes)], axis=1
    )
    total[...] += jnp.dot(
        pair, ritz_ref[...].reshape(2 * lanes, -1), preferred_element_type=f32
    )

    @pl.when(step == pl.num_programs(0) - 1)
    def _():
        out_ref[...] = total[...].astype(bf16).reshape(out_ref.shape)


def projected(cells, ritz, held, chunk, near):
    blocks, rows, vectors, lanes = cells.shape
    kept = ritz.shape[2]
    count = blocks * vectors
    size = count // near
    specs = [
        pl.BlockSpec((blocks, 2, vectors, lanes), lambda r: (0, r, 0, 0)),
        pl.BlockSpec((2, lanes, kept), lambda r: (r, 0, 0)),
    ]
    operands = [cells, ritz]
    if held is not None:
        specs.append(pl.BlockSpec(memory_space=pl.ANY))
        operands.append(held)
    return pl.pallas_call(
        project_kernel,
        out_shape=jax.ShapeDtypeStruct((near, CHUNKS * size, kept), bf16),
        grid=(rows // 2,),
        in_specs=specs,
        out_specs=pl.BlockSpec((near, size, kept), lambda r: (0, chunk, 0)),
        scratch_shapes=[pltpu.VMEM((count, kept), f32)],
        input_output_aliases={} if held is None else {2: 0},
        compiler_params=pltpu.CompilerParams(vmem_limit_bytes=24 << 20),
        cost_estimate=pl.CostEstimate(
            flops=2 * count * rows * lanes * kept, bytes_accessed=7 << 20, transcendentals=0
        ),
    )(*operands)


def remove_kernel(coeffs_ref, ritz_ref, *refs):
    out_ref = refs[-1]
    blocks, rows, vectors, lanes = refs[0].shape

    def remove(cells_ref):
        coeffs = coeffs_ref[...].reshape(blocks * vectors, -1)
        for r in range(0, rows, 2):
            removed = lax.dot_general(
                coeffs,
                ritz_ref[r : r + 2].reshape(2 * lanes, -1),
                (((1,), (1,)), ((), ())),
                preferred_element_type=f32,
            )
            for k in range(2):
                for i in range(blocks):
                    held = cells_ref[i, r + k].astype(f32)
                    part = removed[i * vectors : (i + 1) * vectors, k * lanes : (k + 1) * lanes]
                    out_ref[i, pl.ds(r + k, vectors, stride=rows), :] = held - part

    for k, cells_ref in enumerate(refs[:-1]):
        pl.when(pl.program_id(0) == k)(functools.partial(remove, cells_ref))


def residual(coeffs, ritz, held):
    blocks, rows, vectors, lanes = held[0].shape
    near, _, kept = coeffs.shape
    count = blocks * vectors
    chunks = len(held)
    return pl.pallas_call(
        remove_kernel,
        out_shape=jax.ShapeDtypeStruct((blocks, chunks * vectors * rows, lanes), f32),
        grid=(chunks, PARTS),
        in_specs=[
            pl.BlockSpec((near // PARTS, count // near, kept), lambda k, g: (g, k, 0)),
            pl.BlockSpec((rows, lanes, kept), lambda k, g: (0, 0, 0)),
            *(
                pl.BlockSpec(
                    (blocks // PARTS, rows, vectors, lanes),
                    functools.partial(held_block, own),
                )
                for own in range(chunks)
            ),
        ],
        out_specs=pl.BlockSpec(
            (blocks // PARTS, vectors * rows, lanes), lambda k, g: (g, k, 0)
        ),
        compiler_params=pltpu.CompilerParams(vmem_limit_bytes=32 << 20),
        cost_estimate=pl.CostEstimate(
            flops=2 * chunks * count * rows * lanes * kept,
            bytes_accessed=11 << 20,
            transcendentals=0,
        ),
    )(coeffs, ritz, *held)


def held_block(own, k, g):
    return jnp.where(k == own, g, jnp.where(k < own, 0, PARTS - 1)), 0, 0, 0


def summed(partial):
    blocks = lax.all_to_all(partial, NEAR, 0, 0, tiled=True)
    blocks = jnp.sum(blocks.astype(f32), axis=0)
    blocks = jnp.sum(from_everyone(blocks, LINE), axis=0).astype(bf16)
    return from_everyone(blocks, NEAR)


def from_everyone(value, axis):
    copies = jnp.broadcast_to(value, (lax.axis_size(axis), *value.shape))
    return lax.all_to_all(copies, axis, split_axis=0, concat_axis=0, tiled=True)


def swap_ends(low, high):
    count = lax.axis_size(DOM)
    from_below = lax.ppermute(high, DOM, [(i, i + 1) for i in range(count - 1)])
    from_above = lax.ppermute(low, DOM, [(i + 1, i) for i in range(count - 1)])
    return from_below, from_above


def pipeline(vectors, coefficient, ritz):
    count, planes, rows, lanes = vectors.shape
    size = count // CHUNKS
    below, above = swap_ends(coefficient[:HALO], coefficient[-HALO:])
    diag = jnp.concatenate([below, coefficient, above], axis=0) + (6.0 - 7.125)
    diag = from_everyone(diag, VEC)
    diag = diag.transpose(1, 0, 2, 3).reshape(-1, rows, lanes)
    place = lax.axis_index(DOM)
    ends = jnp.stack([place == 0, place == lax.axis_size(DOM) - 1]).astype(jnp.int32)
    cells = vectors.reshape(count, planes * rows, lanes)
    ritz_rows = pltpu.with_memory_space_constraint(
        ritz.reshape(-1, *ritz.shape[2:]), pltpu.MemorySpace.HBM
    )
    held, total = [], None
    for k in range(CHUNKS):
        low, near, high, far = spread(cells, rows, k, size)
        low, high = swap_ends(low, high)
        blocks = filtered(ends, near, far, low, high, diag)
        held.append(lax.all_to_all(blocks, VEC, 0, 0, tiled=True))
    for k in range(CHUNKS):
        total = projected(held[k], ritz_rows, total, k, lax.axis_size(NEAR))
    coeffs = summed(total)
    out = residual(coeffs, ritz_rows, held)
    return out.reshape(-1, *coefficient.shape)


def solution(mesh):
    fine = Mesh(mesh.devices.reshape(2, 4, 2, 4, 4), ("zh", "x", "c", "y", "zl"))
    placed = (P(VEC, DOM, None, None), P(DOM, VEC, None), P(DOM, VEC, None, None))
    return jax.shard_map(
        pipeline, mesh=fine, in_specs=placed, out_specs=P(None, DOM, VEC, None), check_vma=False
    )
```

```python
import functools

import jax
import jax.numpy as jnp
from jax import lax
from jax.experimental import pallas as pl
from jax.experimental.pallas import tpu as pltpu
from jax.sharding import Mesh, PartitionSpec as P

bf16 = jnp.bfloat16
f32 = jnp.float32

VEC = ("zh", "x", "c")
DOM = ("y", "zl")
SHARE = ("x", "y")
NEAR = ("c", *SHARE)
HALO = 4
GROUP = 16
CHUNKS = 2


def spread_kernel(first_ref, second_ref, low_ref, high_ref):
    for source, target in ((first_ref, low_ref), (second_ref, high_ref)):
        vectors, rows, lanes = source.shape
        flat = source.reshape(vectors * rows, lanes)
        for y in range(rows):
            target[0, y] = flat[pl.ds(y, vectors, stride=rows), :].astype(bf16)


def spread(cells, rows, chunk, size):
    planes, lanes = cells.shape[1] // rows, cells.shape[2]
    half = planes // 2
    out = pl.BlockSpec((1, rows, size, lanes), lambda p: (p, 0, 0, 0))
    return pl.pallas_call(
        spread_kernel,
        out_shape=[jax.ShapeDtypeStruct((half, rows, size, lanes), bf16)] * 2,
        grid=(half,),
        in_specs=[
            pl.BlockSpec((size, rows, lanes), lambda p: (chunk, p, 0)),
            pl.BlockSpec((size, rows, lanes), lambda p: (chunk, p + half, 0)),
        ],
        out_specs=[out] * 2,
        cost_estimate=pl.CostEstimate(
            flops=size * planes * rows * lanes,
            bytes_accessed=6 * size * planes * rows * lanes,
            transcendentals=0,
        ),
    )(cells, cells)


def filter_kernel(ends_ref, own_ref, low_ref, high_ref, diag_ref, out_ref, even, odd):
    total, rows, lanes = diag_ref.shape
    planes = total - 2 * HALO
    flat = own_ref.reshape(GROUP * planes * rows, lanes)
    lane = lax.broadcasted_iota(jnp.int32, (GROUP, lanes), 1)
    first, last = lane == 0, lane == lanes - 1

    def fill(p, carry):
        for y in range(rows):
            even[p, y] = low_ref[p, y].astype(f32)
            even[p + HALO + planes, y] = high_ref[p, y].astype(f32)
        return carry

    lax.fori_loop(0, HALO, fill, 0)

    def copy(p, carry):
        for y in range(rows):
            at = pl.ds(p * rows + y, GROUP, stride=planes * rows)
            even[p + HALO, y] = flat[at, :]
        return carry

    lax.fori_loop(0, planes, copy, 0)

    def step(source, target, weight, reach, scale):
        def plane(p, carry):
            below = None
            here = source[p, 0]
            for y in range(rows):
                above = source[p, y + 1] if y + 1 < rows else None
                left = jnp.where(first, 0.0, pltpu.roll(here, 1, 1))
                right = jnp.where(last, 0.0, pltpu.roll(here, lanes - 1, 1))
                beside = (source[p - 1, y] + source[p + 1, y]) + (left + right)
                if below is not None:
                    beside = beside + below
                if above is not None:
                    beside = beside + above
                value = diag_ref[p, pl.ds(y, 1), :] * here - beside
                if weight:
                    value = value - weight * target[p, y]
                if scale:
                    out_ref[y // 2, 2 * (p - HALO) + y % 2] = (value * scale).astype(bf16)
                else:
                    target[p, y] = value
                below, here = here, above
            return carry

        lax.fori_loop(reach, total - reach, plane, 0)
        if reach < HALO:
            zero = jnp.zeros((GROUP, lanes), f32)

            def clear(at):
                def one(p, carry):
                    for y in range(rows):
                        target[at + p, y] = zero
                    return carry

                lax.fori_loop(0, HALO - reach, one, 0)

            @pl.when(ends_ref[0] == 1)
            def _():
                clear(reach)

            @pl.when(ends_ref[1] == 1)
            def _():
                clear(HALO + planes)

    step(even, odd, 0.0, 1, 0.0)
    step(odd, even, 24.5, 2, 0.0)
    step(even, odd, 12.25, 3, 0.0)
    step(odd, even, 12.25, 4, 8.0 / 2401.0)


def filtered(ends, cells, low, high, diag, chunk, size):
    total, rows, lanes = diag.shape
    planes = total - 2 * HALO
    groups = size // GROUP
    edge = pl.BlockSpec((HALO, rows, GROUP, lanes), lambda g: (0, 0, g, 0))
    return pl.pallas_call(
        filter_kernel,
        out_shape=jax.ShapeDtypeStruct((rows // 2, 2 * planes, size, lanes), bf16),
        grid=(groups,),
        in_specs=[
            pl.BlockSpec(memory_space=pltpu.SMEM),
            pl.BlockSpec((GROUP, planes * rows, lanes), lambda g: (chunk * groups + g, 0, 0)),
            edge,
            edge,
            pl.BlockSpec((total, rows, lanes), lambda g: (0, 0, 0)),
        ],
        out_specs=pl.BlockSpec((rows // 2, 2 * planes, GROUP, lanes), lambda g: (0, 0, g, 0)),
        scratch_shapes=[pltpu.VMEM((total, rows, GROUP, lanes), f32)] * 2,
        compiler_params=pltpu.CompilerParams(vmem_limit_bytes=24 << 20),
        cost_estimate=pl.CostEstimate(
            flops=12 * 44 * rows * size * lanes, bytes_accessed=5 << 20, transcendentals=0
        ),
    )(ends, cells, low, high, diag)


def project_kernel(cells_ref, ritz_ref, *refs):
    out_ref, total = refs[-2:]
    step = pl.program_id(0)
    lanes = cells_ref.shape[3]

    @pl.when(step == 0)
    def _():
        total[...] = jnp.zeros_like(total)

    pair = jnp.concatenate(
        [cells_ref[:, 0].reshape(-1, lanes), cells_ref[:, 1].reshape(-1, lanes)], axis=1
    )
    total[...] += jnp.dot(
        pair, ritz_ref[...].reshape(2 * lanes, -1), preferred_element_type=f32
    )

    @pl.when(step == pl.num_programs(0) - 1)
    def _():
        out_ref[...] = total[...].astype(bf16).reshape(out_ref.shape)


def projected(cells, ritz, held, chunk, near):
    blocks, rows, vectors, lanes = cells.shape
    kept = ritz.shape[2]
    count = blocks * vectors
    size = count // near
    specs = [
        pl.BlockSpec((blocks, 2, vectors, lanes), lambda r: (0, r, 0, 0)),
        pl.BlockSpec((2, lanes, kept), lambda r: (r, 0, 0)),
    ]
    operands = [cells, ritz]
    if held is not None:
        specs.append(pl.BlockSpec(memory_space=pl.ANY))
        operands.append(held)
    return pl.pallas_call(
        project_kernel,
        out_shape=jax.ShapeDtypeStruct((near, CHUNKS * size, kept), bf16),
        grid=(rows // 2,),
        in_specs=specs,
        out_specs=pl.BlockSpec((near, size, kept), lambda r: (0, chunk, 0)),
        scratch_shapes=[pltpu.VMEM((count, kept), f32)],
        input_output_aliases={} if held is None else {2: 0},
        compiler_params=pltpu.CompilerParams(vmem_limit_bytes=24 << 20),
        cost_estimate=pl.CostEstimate(
            flops=2 * count * rows * lanes * kept, bytes_accessed=7 << 20, transcendentals=0
        ),
    )(*operands)


def remove_kernel(core_ref, mine_ref, other_ref, ritz_ref, *refs):
    out_ref = refs[-1]
    blocks, rows, vectors, lanes = refs[0].shape
    mine = mine_ref[...].reshape(blocks * vectors // 2, -1)
    other = other_ref[...].reshape(blocks * vectors // 2, -1)
    first = core_ref[0] == 0
    coeffs = jnp.concatenate(
        [jnp.where(first, mine, other), jnp.where(first, other, mine)], axis=0
    )

    def remove(cells_ref):
        for r in range(0, rows, 2):
            removed = lax.dot_general(
                coeffs,
                ritz_ref[r : r + 2].reshape(2 * lanes, -1),
                (((1,), (1,)), ((), ())),
                preferred_element_type=f32,
            )
            for k in range(2):
                for i in range(blocks):
                    held = cells_ref[i, r + k].astype(f32)
                    part = removed[i * vectors : (i + 1) * vectors, k * lanes : (k + 1) * lanes]
                    out_ref[i, pl.ds(r + k, vectors, stride=rows), :] = held - part

    for k, cells_ref in enumerate(refs[:-1]):
        pl.when(pl.program_id(0) == k)(functools.partial(remove, cells_ref))


def residual(core, mine, other, ritz, held):
    blocks, rows, vectors, lanes = held[0].shape
    near, _, kept = mine.shape
    chunks = len(held)
    size = mine.shape[1] // chunks
    coeffs = pl.BlockSpec((near, size, kept), lambda k: (0, k, 0))
    return pl.pallas_call(
        remove_kernel,
        out_shape=jax.ShapeDtypeStruct((blocks, chunks * vectors * rows, lanes), f32),
        grid=(chunks,),
        in_specs=[
            pl.BlockSpec(memory_space=pltpu.SMEM),
            coeffs,
            coeffs,
            pl.BlockSpec((rows, lanes, kept), lambda k: (0, 0, 0)),
            *([pl.BlockSpec((blocks, rows, vectors, lanes), lambda k: (0, 0, 0, 0))] * chunks),
        ],
        out_specs=pl.BlockSpec((blocks, vectors * rows, lanes), lambda k: (0, k, 0)),
        compiler_params=pltpu.CompilerParams(vmem_limit_bytes=32 << 20),
        cost_estimate=pl.CostEstimate(
            flops=2 * chunks * blocks * vectors * rows * lanes * kept,
            bytes_accessed=11 << 20,
            transcendentals=0,
        ),
    )(core, mine, other, ritz, *held)


def summed(partial):
    blocks = lax.all_to_all(partial, NEAR, 0, 0, tiled=True)
    blocks = jnp.sum(blocks.astype(f32), axis=0)
    blocks = blocks + swapped(blocks, "zh")
    blocks = jnp.sum(from_everyone(blocks, "zl"), axis=0).astype(bf16)
    mine = from_everyone(blocks, SHARE)
    return mine, swapped(mine, "c")


def swapped(value, axis):
    return lax.ppermute(value, axis, [(0, 1), (1, 0)])


def from_everyone(value, axis):
    copies = jnp.broadcast_to(value, (lax.axis_size(axis), *value.shape))
    return lax.all_to_all(copies, axis, split_axis=0, concat_axis=0, tiled=True)


def swap_ends(low, high):
    count = lax.axis_size(DOM)
    from_below = lax.ppermute(high, DOM, [(i, i + 1) for i in range(count - 1)])
    from_above = lax.ppermute(low, DOM, [(i + 1, i) for i in range(count - 1)])
    return from_below, from_above


def pipeline(vectors, coefficient, ritz):
    count, planes, rows, lanes = vectors.shape
    size = count // CHUNKS
    diag = from_everyone(coefficient, VEC)
    diag = diag.transpose(1, 0, 2, 3).reshape(planes, rows, lanes)
    below, above = swap_ends(diag[:HALO], diag[-HALO:])
    diag = jnp.concatenate([below, diag, above], axis=0) + (6.0 - 7.125)
    place = lax.axis_index(DOM)
    ends = jnp.stack([place == 0, place == lax.axis_size(DOM) - 1]).astype(jnp.int32)
    cells = pltpu.with_memory_space_constraint(
        vectors.reshape(count, planes * rows, lanes), pltpu.MemorySpace.HBM
    )
    ritz_rows = pltpu.with_memory_space_constraint(
        ritz.reshape(-1, *ritz.shape[2:]), pltpu.MemorySpace.HBM
    )
    held, total = [], None
    for k in range(CHUNKS):
        low, high = spread(cells, rows, k, size)
        low, high = swap_ends(low, high)
        blocks = filtered(ends, cells, low, high, diag, k, size)
        held.append(lax.all_to_all(blocks, VEC, 0, 0, tiled=True))
    for k in range(CHUNKS):
        total = projected(held[k], ritz_rows, total, k, lax.axis_size(NEAR))
    mine, other = summed(total)
    core = lax.axis_index("c").reshape(1).astype(jnp.int32)
    out = residual(core, mine, other, ritz_rows, held)
    return out.reshape(-1, *coefficient.shape)


def solution(mesh):
    fine = Mesh(mesh.devices.reshape(2, 4, 2, 4, 4), ("zh", "x", "c", "y", "zl"))
    placed = (P(VEC, DOM, None, None), P(DOM, VEC, None), P(DOM, VEC, None, None))
    return jax.shard_map(
        pipeline, mesh=fine, in_specs=placed, out_specs=P(None, DOM, VEC, None), check_vma=False
    )
```

```python
import functools

import jax
import jax.numpy as jnp
from jax import lax
from jax.experimental import pallas as pl
from jax.experimental.pallas import tpu as pltpu
from jax.sharding import Mesh, PartitionSpec as P

bf16 = jnp.bfloat16
f32 = jnp.float32

VEC = ("zh", "x", "c")
DOM = ("y", "zl")
SHARE = ("x", "y")
NEAR = ("c", *SHARE)
HALO = 4
GROUP = 16
CHUNKS = 2


def spread_kernel(first_ref, second_ref, low_ref, high_ref):
    for source, target in ((first_ref, low_ref), (second_ref, high_ref)):
        vectors, rows, lanes = source.shape
        flat = source.reshape(vectors * rows, lanes)
        for y in range(rows):
            target[0, y] = flat[pl.ds(y, vectors, stride=rows), :].astype(bf16)


def spread(cells, rows, chunk, size):
    planes, lanes = cells.shape[1] // rows, cells.shape[2]
    half = planes // 2
    out = pl.BlockSpec((1, rows, size, lanes), lambda p: (p, 0, 0, 0))
    return pl.pallas_call(
        spread_kernel,
        out_shape=[jax.ShapeDtypeStruct((half, rows, size, lanes), bf16)] * 2,
        grid=(half,),
        in_specs=[
            pl.BlockSpec((size, rows, lanes), lambda p: (chunk, p, 0)),
            pl.BlockSpec((size, rows, lanes), lambda p: (chunk, p + half, 0)),
        ],
        out_specs=[out] * 2,
        cost_estimate=pl.CostEstimate(
            flops=size * planes * rows * lanes,
            bytes_accessed=6 * size * planes * rows * lanes,
            transcendentals=0,
        ),
    )(cells, cells)


def filter_kernel(ends_ref, own_ref, low_ref, high_ref, diag_ref, out_ref, even, odd):
    total, rows, lanes = diag_ref.shape
    planes = total - 2 * HALO
    flat = own_ref.reshape(GROUP * planes * rows, lanes)
    lane = lax.broadcasted_iota(jnp.int32, (GROUP, lanes), 1)
    first, last = lane == 0, lane == lanes - 1

    def fill(p, carry):
        for y in range(rows):
            even[p, y] = low_ref[p, y].astype(f32)
            even[p + HALO + planes, y] = high_ref[p, y].astype(f32)
        return carry

    lax.fori_loop(0, HALO, fill, 0)

    def copy(p, carry):
        for y in range(rows):
            at = pl.ds(p * rows + y, GROUP, stride=planes * rows)
            even[p + HALO, y] = flat[at, :]
        return carry

    lax.fori_loop(0, planes, copy, 0)

    def step(source, target, weight, reach, scale):
        def plane(p, carry):
            below = None
            here = source[p, 0]
            for y in range(rows):
                above = source[p, y + 1] if y + 1 < rows else None
                left = jnp.where(first, 0.0, pltpu.roll(here, 1, 1))
                right = jnp.where(last, 0.0, pltpu.roll(here, lanes - 1, 1))
                beside = (source[p - 1, y] + source[p + 1, y]) + (left + right)
                if below is not None:
                    beside = beside + below
                if above is not None:
                    beside = beside + above
                value = diag_ref[p, pl.ds(y, 1), :] * here - beside
                if weight:
                    value = value - weight * target[p, y]
                if scale:
                    out_ref[y // 2, 2 * (p - HALO) + y % 2] = (value * scale).astype(bf16)
                else:
                    target[p, y] = value
                below, here = here, above
            return carry

        lax.fori_loop(reach, total - reach, plane, 0)
        if reach < HALO:
            zero = jnp.zeros((GROUP, lanes), f32)

            def clear(at):
                def one(p, carry):
                    for y in range(rows):
                        target[at + p, y] = zero
                    return carry

                lax.fori_loop(0, HALO - reach, one, 0)

            @pl.when(ends_ref[0] == 1)
            def _():
                clear(reach)

            @pl.when(ends_ref[1] == 1)
            def _():
                clear(HALO + planes)

    step(even, odd, 0.0, 1, 0.0)
    step(odd, even, 24.5, 2, 0.0)
    step(even, odd, 12.25, 3, 0.0)
    step(odd, even, 12.25, 4, 8.0 / 2401.0)


def filtered(ends, cells, low, high, diag, chunk, size):
    total, rows, lanes = diag.shape
    planes = total - 2 * HALO
    groups = size // GROUP
    edge = pl.BlockSpec((HALO, rows, GROUP, lanes), lambda g: (0, 0, g, 0))
    return pl.pallas_call(
        filter_kernel,
        out_shape=jax.ShapeDtypeStruct((rows // 2, 2 * planes, size, lanes), bf16),
        grid=(groups,),
        in_specs=[
            pl.BlockSpec(memory_space=pltpu.SMEM),
            pl.BlockSpec((GROUP, planes * rows, lanes), lambda g: (chunk * groups + g, 0, 0)),
            edge,
            edge,
            pl.BlockSpec((total, rows, lanes), lambda g: (0, 0, 0)),
        ],
        out_specs=pl.BlockSpec((rows // 2, 2 * planes, GROUP, lanes), lambda g: (0, 0, g, 0)),
        scratch_shapes=[pltpu.VMEM((total, rows, GROUP, lanes), f32)] * 2,
        compiler_params=pltpu.CompilerParams(vmem_limit_bytes=24 << 20),
        cost_estimate=pl.CostEstimate(
            flops=12 * 44 * rows * size * lanes, bytes_accessed=5 << 20, transcendentals=0
        ),
    )(ends, cells, low, high, diag)


def project_kernel(cells_ref, ritz_ref, *refs):
    out_ref, total = refs[-2:]
    step = pl.program_id(0)
    lanes = cells_ref.shape[3]

    @pl.when(step == 0)
    def _():
        total[...] = jnp.zeros_like(total)

    pair = jnp.concatenate(
        [cells_ref[:, 0].reshape(-1, lanes), cells_ref[:, 1].reshape(-1, lanes)], axis=1
    )
    total[...] += jnp.dot(
        pair, ritz_ref[...].reshape(2 * lanes, -1), preferred_element_type=f32
    )

    @pl.when(step == pl.num_programs(0) - 1)
    def _():
        out_ref[...] = total[...].astype(bf16).reshape(out_ref.shape)


def projected(cells, ritz, held, chunk, near):
    blocks, rows, vectors, lanes = cells.shape
    kept = ritz.shape[2]
    count = blocks * vectors
    size = count // near
    specs = [
        pl.BlockSpec((blocks, 2, vectors, lanes), lambda r: (0, r, 0, 0)),
        pl.BlockSpec((2, lanes, kept), lambda r: (r, 0, 0)),
    ]
    operands = [cells, ritz]
    if held is not None:
        specs.append(pl.BlockSpec(memory_space=pl.ANY))
        operands.append(held)
    return pl.pallas_call(
        project_kernel,
        out_shape=jax.ShapeDtypeStruct((near, CHUNKS * size, kept), bf16),
        grid=(rows // 2,),
        in_specs=specs,
        out_specs=pl.BlockSpec((near, size, kept), lambda r: (0, chunk, 0)),
        scratch_shapes=[pltpu.VMEM((count, kept), f32)],
        input_output_aliases={} if held is None else {2: 0},
        compiler_params=pltpu.CompilerParams(vmem_limit_bytes=24 << 20),
        cost_estimate=pl.CostEstimate(
            flops=2 * count * rows * lanes * kept, bytes_accessed=7 << 20, transcendentals=0
        ),
    )(*operands)


def remove_kernel(core_ref, mine_ref, other_ref, ritz_ref, *refs):
    out_ref = refs[-1]
    blocks, rows, vectors, lanes = refs[0].shape
    mine = mine_ref[...].reshape(blocks * vectors // 2, -1)
    other = other_ref[...].reshape(blocks * vectors // 2, -1)
    first = core_ref[0] == 0
    coeffs = jnp.concatenate(
        [jnp.where(first, mine, other), jnp.where(first, other, mine)], axis=0
    )

    def remove(cells_ref):
        for r in range(0, rows, 2):
            removed = lax.dot_general(
                coeffs,
                ritz_ref[r : r + 2].reshape(2 * lanes, -1),
                (((1,), (1,)), ((), ())),
                preferred_element_type=f32,
            )
            for k in range(2):
                for i in range(blocks):
                    held = cells_ref[i, r + k].astype(f32)
                    part = removed[i * vectors : (i + 1) * vectors, k * lanes : (k + 1) * lanes]
                    out_ref[i, pl.ds(r + k, vectors, stride=rows), :] = held - part

    for k, cells_ref in enumerate(refs[:-1]):
        pl.when(pl.program_id(0) == k)(functools.partial(remove, cells_ref))


def residual(core, mine, other, ritz, held):
    blocks, rows, vectors, lanes = held[0].shape
    near, _, kept = mine.shape
    chunks = len(held)
    size = mine.shape[1] // chunks
    coeffs = pl.BlockSpec((near, size, kept), lambda k: (0, k, 0))
    return pl.pallas_call(
        remove_kernel,
        out_shape=jax.ShapeDtypeStruct((blocks, chunks * vectors * rows, lanes), f32),
        grid=(chunks,),
        in_specs=[
            pl.BlockSpec(memory_space=pltpu.SMEM),
            coeffs,
            coeffs,
            pl.BlockSpec((rows, lanes, kept), lambda k: (0, 0, 0)),
            *([pl.BlockSpec((blocks, rows, vectors, lanes), lambda k: (0, 0, 0, 0))] * chunks),
        ],
        out_specs=pl.BlockSpec((blocks, vectors * rows, lanes), lambda k: (0, k, 0)),
        compiler_params=pltpu.CompilerParams(vmem_limit_bytes=32 << 20),
        cost_estimate=pl.CostEstimate(
            flops=2 * chunks * blocks * vectors * rows * lanes * kept,
            bytes_accessed=11 << 20,
            transcendentals=0,
        ),
    )(core, mine, other, ritz, *held)


def summed(partial):
    blocks = lax.all_to_all(partial, NEAR, 0, 0, tiled=True)
    blocks = jnp.sum(blocks.astype(f32), axis=0)
    blocks = blocks + swapped(blocks, "zh")
    count = lax.axis_size("zl")
    terms = [blocks] + [
        lax.ppermute(blocks, "zl", [(i, i ^ k) for i in range(count)])
        for k in range(1, count)
    ]
    while len(terms) > 1:
        terms = [a + b for a, b in zip(terms[::2], terms[1::2])]
    blocks = terms[0].astype(bf16)
    mine = from_everyone(blocks, SHARE)
    return mine, swapped(mine, "c")


def swapped(value, axis):
    return lax.ppermute(value, axis, [(0, 1), (1, 0)])


def from_everyone(value, axis):
    copies = jnp.broadcast_to(value, (lax.axis_size(axis), *value.shape))
    return lax.all_to_all(copies, axis, split_axis=0, concat_axis=0, tiled=True)


def swap_ends(low, high):
    count = lax.axis_size(DOM)
    from_below = lax.ppermute(high, DOM, [(i, i + 1) for i in range(count - 1)])
    from_above = lax.ppermute(low, DOM, [(i + 1, i) for i in range(count - 1)])
    return from_below, from_above


def pipeline(vectors, coefficient, ritz):
    count, planes, rows, lanes = vectors.shape
    size = count // CHUNKS
    below, above = swap_ends(coefficient[:HALO], coefficient[-HALO:])
    diag = jnp.concatenate([below, coefficient, above], axis=0) + (6.0 - 7.125)
    other = swapped(diag, "zh")
    first = lax.axis_index("zh") == 0
    diag = jnp.stack([jnp.where(first, diag, other), jnp.where(first, other, diag)])
    diag = from_everyone(diag, ("x", "c"))
    diag = diag.transpose(2, 1, 0, 3, 4).reshape(-1, rows, lanes)
    place = lax.axis_index(DOM)
    ends = jnp.stack([place == 0, place == lax.axis_size(DOM) - 1]).astype(jnp.int32)
    cells = pltpu.with_memory_space_constraint(
        vectors.reshape(count, planes * rows, lanes), pltpu.MemorySpace.HBM
    )
    ritz_rows = pltpu.with_memory_space_constraint(
        ritz.reshape(-1, *ritz.shape[2:]), pltpu.MemorySpace.HBM
    )
    held, total = [], None
    for k in range(CHUNKS):
        low, high = spread(cells, rows, k, size)
        low, high = swap_ends(low, high)
        blocks = filtered(ends, cells, low, high, diag, k, size)
        held.append(lax.all_to_all(blocks, VEC, 0, 0, tiled=True))
    for k in range(CHUNKS):
        total = projected(held[k], ritz_rows, total, k, lax.axis_size(NEAR))
    mine, other = summed(total)
    core = lax.axis_index("c").reshape(1).astype(jnp.int32)
    out = residual(core, mine, other, ritz_rows, held)
    return out.reshape(-1, *coefficient.shape)


def solution(mesh):
    fine = Mesh(mesh.devices.reshape(2, 4, 2, 4, 4), ("zh", "x", "c", "y", "zl"))
    placed = (P(VEC, DOM, None, None), P(DOM, VEC, None), P(DOM, VEC, None, None))
    return jax.shard_map(
        pipeline, mesh=fine, in_specs=placed, out_specs=P(None, DOM, VEC, None), check_vma=False
    )
```

```python
import functools

import jax
import jax.numpy as jnp
from jax import lax
from jax.experimental import pallas as pl
from jax.experimental.pallas import tpu as pltpu
from jax.sharding import Mesh, PartitionSpec as P

bf16 = jnp.bfloat16
f32 = jnp.float32

VEC = ("zh", "x", "c")
DOM = ("y", "zl")
SHARE = ("x", "y")
NEAR = ("c", *SHARE)
HALO = 4
GROUP = 16
CHUNKS = 2


def spread_kernel(first_ref, second_ref, low_ref, high_ref):
    for source, target in ((first_ref, low_ref), (second_ref, high_ref)):
        vectors, rows, lanes = source.shape
        flat = source.reshape(vectors * rows, lanes)
        for y in range(rows):
            target[0, y] = flat[pl.ds(y, vectors, stride=rows), :].astype(bf16)


def spread(cells, rows, chunk, size):
    planes, lanes = cells.shape[1] // rows, cells.shape[2]
    half = planes // 2
    out = pl.BlockSpec((1, rows, size, lanes), lambda p: (p, 0, 0, 0))
    return pl.pallas_call(
        spread_kernel,
        out_shape=[jax.ShapeDtypeStruct((half, rows, size, lanes), bf16)] * 2,
        grid=(half,),
        in_specs=[
            pl.BlockSpec((size, rows, lanes), lambda p: (chunk, p, 0)),
            pl.BlockSpec((size, rows, lanes), lambda p: (chunk, p + half, 0)),
        ],
        out_specs=[out] * 2,
        cost_estimate=pl.CostEstimate(
            flops=size * planes * rows * lanes,
            bytes_accessed=6 * size * planes * rows * lanes,
            transcendentals=0,
        ),
    )(cells, cells)


def filter_kernel(ends_ref, own_ref, low_ref, high_ref, diag_ref, out_ref, even, odd):
    total, rows, lanes = diag_ref.shape
    planes = total - 2 * HALO
    flat = own_ref.reshape(GROUP * planes * rows, lanes)
    lane = lax.broadcasted_iota(jnp.int32, (GROUP, lanes), 1)
    first, last = lane == 0, lane == lanes - 1

    def fill(p, carry):
        for y in range(rows):
            even[p, y] = low_ref[p, y].astype(f32)
            even[p + HALO + planes, y] = high_ref[p, y].astype(f32)
        return carry

    lax.fori_loop(0, HALO, fill, 0)

    def copy(p, carry):
        for y in range(rows):
            at = pl.ds(p * rows + y, GROUP, stride=planes * rows)
            even[p + HALO, y] = flat[at, :]
        return carry

    lax.fori_loop(0, planes, copy, 0)

    def step(source, target, weight, reach, scale):
        def plane(p, carry):
            below = None
            here = source[p, 0]
            for y in range(rows):
                above = source[p, y + 1] if y + 1 < rows else None
                left = jnp.where(first, 0.0, pltpu.roll(here, 1, 1))
                right = jnp.where(last, 0.0, pltpu.roll(here, lanes - 1, 1))
                beside = (source[p - 1, y] + source[p + 1, y]) + (left + right)
                if below is not None:
                    beside = beside + below
                if above is not None:
                    beside = beside + above
                value = diag_ref[p, pl.ds(y, 1), :] * here - beside
                if weight:
                    value = value - weight * target[p, y]
                if scale:
                    out_ref[y // 2, 2 * (p - HALO) + y % 2] = (value * scale).astype(bf16)
                else:
                    target[p, y] = value
                below, here = here, above
            return carry

        lax.fori_loop(reach, total - reach, plane, 0)
        if reach < HALO:
            zero = jnp.zeros((GROUP, lanes), f32)

            def clear(at):
                def one(p, carry):
                    for y in range(rows):
                        target[at + p, y] = zero
                    return carry

                lax.fori_loop(0, HALO - reach, one, 0)

            @pl.when(ends_ref[0] == 1)
            def _():
                clear(reach)

            @pl.when(ends_ref[1] == 1)
            def _():
                clear(HALO + planes)

    step(even, odd, 0.0, 1, 0.0)
    step(odd, even, 24.5, 2, 0.0)
    step(even, odd, 12.25, 3, 0.0)
    step(odd, even, 12.25, 4, 8.0 / 2401.0)


def split_filter_kernel(ends_ref, own_ref, low_ref, high_ref, diag_ref, *refs):
    *out_refs, even, odd, blocks, sems = refs
    filter_kernel(ends_ref, own_ref, low_ref, high_ref, diag_ref, blocks, even, odd)
    copies = [
        pltpu.make_async_copy(blocks.at[ends_ref[2] ^ k], out_ref, sems.at[k])
        for k, out_ref in enumerate(out_refs)
    ]
    for copy in copies:
        copy.start()
    for copy in copies:
        copy.wait()


def filtered(ends, cells, low, high, diag, chunk, size, split):
    total, rows, lanes = diag.shape
    planes = total - 2 * HALO
    groups = size // GROUP
    edge = pl.BlockSpec((HALO, rows, GROUP, lanes), lambda g: (0, 0, g, 0))
    count, shape = rows // 2, (2 * planes, GROUP, lanes)
    scratch = [pltpu.VMEM((total, rows, GROUP, lanes), f32)] * 2
    if split:
        out_shape = [jax.ShapeDtypeStruct(shape, bf16)] * count
        out_specs = [pl.BlockSpec(memory_space=pl.ANY)] * count
        scratch += [pltpu.VMEM((count, *shape), bf16), pltpu.SemaphoreType.DMA((count,))]
    else:
        out_shape = jax.ShapeDtypeStruct((count, 2 * planes, size, lanes), bf16)
        out_specs = pl.BlockSpec((count, *shape), lambda g: (0, 0, g, 0))
    return pl.pallas_call(
        split_filter_kernel if split else filter_kernel,
        out_shape=out_shape,
        grid=(groups,),
        in_specs=[
            pl.BlockSpec(memory_space=pltpu.SMEM),
            pl.BlockSpec((GROUP, planes * rows, lanes), lambda g: (chunk * groups + g, 0, 0)),
            edge,
            edge,
            pl.BlockSpec((total, rows, lanes), lambda g: (0, 0, 0)),
        ],
        out_specs=out_specs,
        scratch_shapes=scratch,
        compiler_params=pltpu.CompilerParams(vmem_limit_bytes=24 << 20),
        cost_estimate=pl.CostEstimate(
            flops=12 * 44 * rows * size * lanes, bytes_accessed=5 << 20, transcendentals=0
        ),
    )(ends, cells, low, high, diag)


def project_kernel(ritz_ref, cells_ref, out_ref, total):
    lanes = cells_ref.shape[3]
    pair = jnp.concatenate(
        [cells_ref[:, 0].reshape(-1, lanes), cells_ref[:, 1].reshape(-1, lanes)], axis=1
    )
    accumulate(pair, ritz_ref, out_ref, total)


def accumulate(pair, ritz_ref, out_ref, total):
    step = pl.program_id(0)

    @pl.when(step == 0)
    def _():
        total[...] = jnp.zeros_like(total)

    total[...] += jnp.dot(
        pair, ritz_ref[...].reshape(pair.shape[1], -1), preferred_element_type=f32
    )

    @pl.when(step == pl.num_programs(0) - 1)
    def _():
        out_ref[...] = total[...].astype(bf16).reshape(out_ref.shape)


def joined_project_kernel(place_ref, ritz_ref, *refs):
    *block_refs, out_ref, held_ref, total, pairs = refs
    for k, block_ref in enumerate(block_refs):
        source = place_ref[0] ^ k
        held_ref[source] = block_ref[...]
        pairs[source] = jnp.concatenate([block_ref[0], block_ref[1]], axis=1)
    accumulate(pairs[...].reshape(-1, pairs.shape[2]), ritz_ref, out_ref, total)


def projected(cells, ritz, near, place):
    joined = isinstance(cells, list)
    blocks = len(cells)
    rows, vectors, lanes = cells[0].shape
    kept = ritz.shape[2]
    count = blocks * vectors
    out_shape = [jax.ShapeDtypeStruct((near, count // near, kept), bf16)]
    out_specs = [pl.BlockSpec((near, count // near, kept), lambda r: (0, 0, 0))]
    in_specs = [pl.BlockSpec((2, lanes, kept), lambda r: (r, 0, 0))]
    scratch = [pltpu.VMEM((count, kept), f32)]
    block = pl.BlockSpec((blocks, 2, vectors, lanes), lambda r: (0, r, 0, 0))
    if joined:
        in_specs.insert(0, pl.BlockSpec(memory_space=pltpu.SMEM))
        in_specs += [pl.BlockSpec((2, vectors, lanes), lambda r: (r, 0, 0))] * blocks
        out_shape.append(jax.ShapeDtypeStruct((blocks, rows, vectors, lanes), bf16))
        out_specs.append(block)
        scratch.append(pltpu.VMEM((blocks, vectors, 2 * lanes), bf16))
        operands = [place, ritz, *cells]
    else:
        in_specs.append(block)
        operands = [ritz, cells]
    out = pl.pallas_call(
        joined_project_kernel if joined else project_kernel,
        out_shape=out_shape,
        grid=(rows // 2,),
        in_specs=in_specs,
        out_specs=out_specs,
        scratch_shapes=scratch,
        compiler_params=pltpu.CompilerParams(vmem_limit_bytes=24 << 20),
        cost_estimate=pl.CostEstimate(
            flops=2 * count * rows * lanes * kept, bytes_accessed=7 << 20, transcendentals=0
        ),
    )(*operands)
    return (out[0], out[1]) if joined else (out[0], cells)


def remove_kernel(core_ref, mine_ref, other_ref, ritz_ref, *refs):
    out_ref = refs[-1]
    blocks, rows, vectors, lanes = refs[0].shape
    mine = mine_ref[...].reshape(blocks * vectors // 2, -1)
    other = other_ref[...].reshape(blocks * vectors // 2, -1)
    first = core_ref[0] == 0
    coeffs = jnp.concatenate(
        [jnp.where(first, mine, other), jnp.where(first, other, mine)], axis=0
    )

    def remove(cells_ref):
        for r in range(0, rows, 2):
            removed = lax.dot_general(
                coeffs,
                ritz_ref[r : r + 2].reshape(2 * lanes, -1),
                (((1,), (1,)), ((), ())),
                preferred_element_type=f32,
            )
            for k in range(2):
                for i in range(blocks):
                    held = cells_ref[i, r + k].astype(f32)
                    part = removed[i * vectors : (i + 1) * vectors, k * lanes : (k + 1) * lanes]
                    out_ref[i, pl.ds(r + k, vectors, stride=rows), :] = held - part

    for k, cells_ref in enumerate(refs[:-1]):
        pl.when(pl.program_id(0) == k)(functools.partial(remove, cells_ref))


def residual(core, mine, other, ritz, held):
    blocks, rows, vectors, lanes = held[0].shape
    near, _, kept = mine.shape
    chunks = len(held)
    size = mine.shape[1] // chunks
    coeffs = pl.BlockSpec((near, size, kept), lambda k: (0, k, 0))
    return pl.pallas_call(
        remove_kernel,
        out_shape=jax.ShapeDtypeStruct((blocks, chunks * vectors * rows, lanes), f32),
        grid=(chunks,),
        in_specs=[
            pl.BlockSpec(memory_space=pltpu.SMEM),
            coeffs,
            coeffs,
            pl.BlockSpec((rows, lanes, kept), lambda k: (0, 0, 0)),
            *([pl.BlockSpec((blocks, rows, vectors, lanes), lambda k: (0, 0, 0, 0))] * chunks),
        ],
        out_specs=pl.BlockSpec((blocks, vectors * rows, lanes), lambda k: (0, k, 0)),
        compiler_params=pltpu.CompilerParams(vmem_limit_bytes=32 << 20),
        cost_estimate=pl.CostEstimate(
            flops=2 * chunks * blocks * vectors * rows * lanes * kept,
            bytes_accessed=11 << 20,
            transcendentals=0,
        ),
    )(core, mine, other, ritz, *held)


def exchanged(blocks, axis):
    size = len(blocks)
    half = size // 2
    received = list(blocks)
    for k in [*range(half, size), *range(1, half)]:
        received[k] = lax.ppermute(blocks[k], axis, [(i, i ^ k) for i in range(size)])
    return received


def near_sum(partial):
    blocks = lax.all_to_all(partial, NEAR, 0, 0, tiled=True)
    return jnp.sum(blocks.astype(f32), axis=0)


def summed(parts):
    blocks = jnp.concatenate(parts, axis=0)
    blocks = blocks + swapped(blocks, "zh")
    count = lax.axis_size("zl")
    terms = [blocks] + [
        lax.ppermute(blocks, "zl", [(i, i ^ k) for i in range(count)])
        for k in range(1, count)
    ]
    while len(terms) > 1:
        terms = [a + b for a, b in zip(terms[::2], terms[1::2])]
    blocks = terms[0].astype(bf16)
    mine = from_everyone(blocks, SHARE)
    return mine, swapped(mine, "c")


def swapped(value, axis):
    return lax.ppermute(value, axis, [(0, 1), (1, 0)])


def from_everyone(value, axis):
    copies = jnp.broadcast_to(value, (lax.axis_size(axis), *value.shape))
    return lax.all_to_all(copies, axis, split_axis=0, concat_axis=0, tiled=True)


def swap_ends(low, high):
    count = lax.axis_size(DOM)
    from_below = lax.ppermute(high, DOM, [(i, i + 1) for i in range(count - 1)])
    from_above = lax.ppermute(low, DOM, [(i + 1, i) for i in range(count - 1)])
    return from_below, from_above


def pipeline(vectors, coefficient, ritz):
    count, planes, rows, lanes = vectors.shape
    size = count // CHUNKS
    below, above = swap_ends(coefficient[:HALO], coefficient[-HALO:])
    diag = jnp.concatenate([below, coefficient, above], axis=0) + (6.0 - 7.125)
    other = swapped(diag, "zh")
    first = lax.axis_index("zh") == 0
    diag = jnp.stack([jnp.where(first, diag, other), jnp.where(first, other, diag)])
    diag = from_everyone(diag, ("x", "c"))
    diag = diag.transpose(2, 1, 0, 3, 4).reshape(-1, rows, lanes)
    place = lax.axis_index(DOM)
    column = lax.axis_index(VEC).astype(jnp.int32)
    ends = jnp.stack([place == 0, place == lax.axis_size(DOM) - 1]).astype(jnp.int32)
    ends = jnp.concatenate([ends, column.reshape(1)])
    cells = pltpu.with_memory_space_constraint(
        vectors.reshape(count, planes * rows, lanes), pltpu.MemorySpace.HBM
    )
    ritz_rows = pltpu.with_memory_space_constraint(
        ritz.reshape(-1, *ritz.shape[2:]), pltpu.MemorySpace.HBM
    )
    held, parts = [], []
    for k in range(CHUNKS):
        last = k == CHUNKS - 1
        low, high = spread(cells, rows, k, size)
        low, high = swap_ends(low, high)
        blocks = filtered(ends, cells, low, high, diag, k, size, last)
        if last:
            held.append(exchanged(list(blocks), VEC))
        else:
            held.append(lax.all_to_all(blocks, VEC, 0, 0, tiled=True))
    for k in range(CHUNKS):
        partial, held[k] = projected(
            held[k], ritz_rows, lax.axis_size(NEAR), column.reshape(1)
        )
        parts.append(near_sum(partial))
    mine, other = summed(parts)
    core = lax.axis_index("c").reshape(1).astype(jnp.int32)
    out = residual(core, mine, other, ritz_rows, held)
    return out.reshape(-1, *coefficient.shape)


def solution(mesh):
    fine = Mesh(mesh.devices.reshape(2, 4, 2, 4, 4), ("zh", "x", "c", "y", "zl"))
    placed = (P(VEC, DOM, None, None), P(DOM, VEC, None), P(DOM, VEC, None, None))
    return jax.shard_map(
        pipeline, mesh=fine, in_specs=placed, out_specs=P(None, DOM, VEC, None), check_vma=False
    )
```

```python
import functools

import jax
import jax.numpy as jnp
from jax import lax
from jax.experimental import pallas as pl
from jax.experimental.pallas import tpu as pltpu
from jax.sharding import Mesh, PartitionSpec as P

bf16 = jnp.bfloat16
f32 = jnp.float32

VEC = ("zh", "x", "c")
DOM = ("y", "zl")
SHARE = ("y", "x")
NEAR = ("c", *SHARE)
HALO = 4
GROUP = 16
CHUNKS = 2


def spread_kernel(first_ref, second_ref, low_ref, high_ref):
    for source, target in ((first_ref, low_ref), (second_ref, high_ref)):
        vectors, rows, lanes = source.shape
        flat = source.reshape(vectors * rows, lanes)
        for y in range(rows):
            target[0, y] = flat[pl.ds(y, vectors, stride=rows), :].astype(bf16)


def spread(cells, rows, chunk, size):
    planes, lanes = cells.shape[1] // rows, cells.shape[2]
    half = planes // 2
    out = pl.BlockSpec((1, rows, size, lanes), lambda p: (p, 0, 0, 0))
    return pl.pallas_call(
        spread_kernel,
        out_shape=[jax.ShapeDtypeStruct((half, rows, size, lanes), bf16)] * 2,
        grid=(half,),
        in_specs=[
            pl.BlockSpec((size, rows, lanes), lambda p: (chunk, p, 0)),
            pl.BlockSpec((size, rows, lanes), lambda p: (chunk, p + half, 0)),
        ],
        out_specs=[out] * 2,
        cost_estimate=pl.CostEstimate(
            flops=size * planes * rows * lanes,
            bytes_accessed=6 * size * planes * rows * lanes,
            transcendentals=0,
        ),
    )(cells, cells)


def filter_kernel(ends_ref, own_ref, low_ref, high_ref, diag_ref, out_ref, even, odd):
    total, rows, lanes = diag_ref.shape
    planes = total - 2 * HALO
    flat = own_ref.reshape(GROUP * planes * rows, lanes)
    lane = lax.broadcasted_iota(jnp.int32, (GROUP, lanes), 1)
    first, last = lane == 0, lane == lanes - 1

    def fill(p, carry):
        for y in range(rows):
            even[p, y] = low_ref[p, y].astype(f32)
            even[p + HALO + planes, y] = high_ref[p, y].astype(f32)
        return carry

    lax.fori_loop(0, HALO, fill, 0)

    def copy(p, carry):
        for y in range(rows):
            at = pl.ds(p * rows + y, GROUP, stride=planes * rows)
            even[p + HALO, y] = flat[at, :]
        return carry

    lax.fori_loop(0, planes, copy, 0)

    def step(source, target, weight, reach, scale):
        def plane(p, carry):
            below = None
            here = source[p, 0]
            for y in range(rows):
                above = source[p, y + 1] if y + 1 < rows else None
                left = jnp.where(first, 0.0, pltpu.roll(here, 1, 1))
                right = jnp.where(last, 0.0, pltpu.roll(here, lanes - 1, 1))
                beside = (source[p - 1, y] + source[p + 1, y]) + (left + right)
                if below is not None:
                    beside = beside + below
                if above is not None:
                    beside = beside + above
                value = diag_ref[p, pl.ds(y, 1), :] * here - beside
                if weight:
                    value = value - weight * target[p, y]
                if scale:
                    out_ref[y // 2, 2 * (p - HALO) + y % 2] = (value * scale).astype(bf16)
                else:
                    target[p, y] = value
                below, here = here, above
            return carry

        lax.fori_loop(reach, total - reach, plane, 0)
        if reach < HALO:
            zero = jnp.zeros((GROUP, lanes), f32)

            def clear(at):
                def one(p, carry):
                    for y in range(rows):
                        target[at + p, y] = zero
                    return carry

                lax.fori_loop(0, HALO - reach, one, 0)

            @pl.when(ends_ref[0] == 1)
            def _():
                clear(reach)

            @pl.when(ends_ref[1] == 1)
            def _():
                clear(HALO + planes)

    step(even, odd, 0.0, 1, 0.0)
    step(odd, even, 24.5, 2, 0.0)
    step(even, odd, 12.25, 3, 0.0)
    step(odd, even, 12.25, 4, 8.0 / 2401.0)


def filtered(ends, cells, low, high, diag, chunk, size):
    total, rows, lanes = diag.shape
    planes = total - 2 * HALO
    groups = size // GROUP
    edge = pl.BlockSpec((HALO, rows, GROUP, lanes), lambda g: (0, 0, g, 0))
    return pl.pallas_call(
        filter_kernel,
        out_shape=jax.ShapeDtypeStruct((rows // 2, 2 * planes, size, lanes), bf16),
        grid=(groups,),
        in_specs=[
            pl.BlockSpec(memory_space=pltpu.SMEM),
            pl.BlockSpec((GROUP, planes * rows, lanes), lambda g: (chunk * groups + g, 0, 0)),
            edge,
            edge,
            pl.BlockSpec((total, rows, lanes), lambda g: (0, 0, 0)),
        ],
        out_specs=pl.BlockSpec((rows // 2, 2 * planes, GROUP, lanes), lambda g: (0, 0, g, 0)),
        scratch_shapes=[pltpu.VMEM((total, rows, GROUP, lanes), f32)] * 2,
        compiler_params=pltpu.CompilerParams(vmem_limit_bytes=24 << 20),
        cost_estimate=pl.CostEstimate(
            flops=12 * 44 * rows * size * lanes, bytes_accessed=5 << 20, transcendentals=0
        ),
    )(ends, cells, low, high, diag)


def project_kernel(place_ref, ritz_ref, cells_ref, out_ref, total):
    step = pl.program_id(0)
    lanes = cells_ref.shape[3]

    @pl.when(step == 0)
    def _():
        total[...] = jnp.zeros_like(total)

    pair = jnp.concatenate(
        [cells_ref[:, 0].reshape(-1, lanes), cells_ref[:, 1].reshape(-1, lanes)], axis=1
    )
    total[...] += jnp.dot(
        pair, ritz_ref[...].reshape(2 * lanes, -1), preferred_element_type=f32
    )

    @pl.when(step == pl.num_programs(0) - 1)
    def _():
        near, size, _ = out_ref.shape
        if out_ref.dtype == f32:
            for q in range(near):
                out_ref[place_ref[0] ^ q] = total[q * size : (q + 1) * size, :]
        else:
            out_ref[...] = total[...].astype(bf16).reshape(out_ref.shape)


def projected(cells, ritz, near, place, kind):
    blocks, rows, vectors, lanes = cells.shape
    kept = ritz.shape[2]
    count = blocks * vectors
    return pl.pallas_call(
        project_kernel,
        out_shape=jax.ShapeDtypeStruct((near, count // near, kept), kind),
        grid=(rows // 2,),
        in_specs=[
            pl.BlockSpec(memory_space=pltpu.SMEM),
            pl.BlockSpec((2, lanes, kept), lambda r: (r, 0, 0)),
            pl.BlockSpec((blocks, 2, vectors, lanes), lambda r: (0, r, 0, 0)),
        ],
        out_specs=pl.BlockSpec((near, count // near, kept), lambda r: (0, 0, 0)),
        scratch_shapes=[pltpu.VMEM((count, kept), f32)],
        compiler_params=pltpu.CompilerParams(vmem_limit_bytes=24 << 20),
        cost_estimate=pl.CostEstimate(
            flops=2 * count * rows * lanes * kept, bytes_accessed=7 << 20, transcendentals=0
        ),
    )(place, ritz, cells)


def remove_kernel(core_ref, mine_ref, other_ref, ritz_ref, *refs):
    out_ref = refs[-1]
    blocks, rows, vectors, lanes = refs[0].shape
    mine = mine_ref[...].reshape(blocks * vectors // 2, -1)
    other = other_ref[...].reshape(blocks * vectors // 2, -1)
    first = core_ref[0] == 0
    coeffs = jnp.concatenate(
        [jnp.where(first, mine, other), jnp.where(first, other, mine)], axis=0
    )

    def remove(cells_ref):
        for r in range(0, rows, 2):
            removed = lax.dot_general(
                coeffs,
                ritz_ref[r : r + 2].reshape(2 * lanes, -1),
                (((1,), (1,)), ((), ())),
                preferred_element_type=f32,
            )
            for k in range(2):
                for i in range(blocks):
                    held = cells_ref[i, r + k].astype(f32)
                    part = removed[i * vectors : (i + 1) * vectors, k * lanes : (k + 1) * lanes]
                    out_ref[i, pl.ds(r + k, vectors, stride=rows), :] = held - part

    for k, cells_ref in enumerate(refs[:-1]):
        pl.when(pl.program_id(0) == k)(functools.partial(remove, cells_ref))


def residual(core, mine, other, ritz, held):
    blocks, rows, vectors, lanes = held[0].shape
    near, _, kept = mine.shape
    chunks = len(held)
    size = mine.shape[1] // chunks
    coeffs = pl.BlockSpec((near, size, kept), lambda k: (0, k, 0))
    return pl.pallas_call(
        remove_kernel,
        out_shape=jax.ShapeDtypeStruct((blocks, chunks * vectors * rows, lanes), f32),
        grid=(chunks,),
        in_specs=[
            pl.BlockSpec(memory_space=pltpu.SMEM),
            coeffs,
            coeffs,
            pl.BlockSpec((rows, lanes, kept), lambda k: (0, 0, 0)),
            *([pl.BlockSpec((blocks, rows, vectors, lanes), lambda k: (0, 0, 0, 0))] * chunks),
        ],
        out_specs=pl.BlockSpec((blocks, vectors * rows, lanes), lambda k: (0, k, 0)),
        compiler_params=pltpu.CompilerParams(vmem_limit_bytes=32 << 20),
        cost_estimate=pl.CostEstimate(
            flops=2 * chunks * blocks * vectors * rows * lanes * kept,
            bytes_accessed=11 << 20,
            transcendentals=0,
        ),
    )(core, mine, other, ritz, *held)


def total_of(terms):
    while len(terms) > 1:
        terms = [a + b for a, b in zip(terms[::2], terms[1::2])]
    return terms[0]


def traded(blocks, axis):
    count = lax.axis_size(axis)
    return total_of(
        [blocks[0]]
        + [
            lax.ppermute(blocks[k], axis, [(i, i ^ k) for i in range(count)])
            for k in range(1, count)
        ]
    )


def near_sum(partial):
    if partial.dtype == bf16:
        blocks = lax.all_to_all(partial, NEAR, 0, 0, tiled=True)
        return jnp.sum(blocks.astype(f32), axis=0)
    for axis in NEAR:
        count = lax.axis_size(axis)
        partial = traded(partial.reshape(count, -1, *partial.shape[-2:]), axis)
    return partial[0]


def summed(parts):
    blocks = jnp.concatenate(parts, axis=0)
    blocks = blocks + swapped(blocks, "zh")
    blocks = traded([blocks] * lax.axis_size("zl"), "zl").astype(bf16)
    mine = from_everyone(blocks, SHARE)
    return mine, swapped(mine, "c")


def swapped(value, axis):
    return lax.ppermute(value, axis, [(0, 1), (1, 0)])


def from_everyone(value, axis):
    copies = jnp.broadcast_to(value, (lax.axis_size(axis), *value.shape))
    return lax.all_to_all(copies, axis, split_axis=0, concat_axis=0, tiled=True)


def swap_ends(low, high):
    count = lax.axis_size(DOM)
    from_below = lax.ppermute(high, DOM, [(i, i + 1) for i in range(count - 1)])
    from_above = lax.ppermute(low, DOM, [(i + 1, i) for i in range(count - 1)])
    return from_below, from_above


def pipeline(vectors, coefficient, ritz):
    count, planes, rows, lanes = vectors.shape
    size = count // CHUNKS
    other = swapped(coefficient, "zh")
    first = lax.axis_index("zh") == 0
    diag = jnp.stack(
        [jnp.where(first, coefficient, other), jnp.where(first, other, coefficient)]
    )
    diag = from_everyone(diag, ("x", "c"))
    diag = diag.transpose(2, 1, 0, 3, 4).reshape(planes, rows, lanes) + (6.0 - 7.125)
    below, above = swap_ends(diag[:HALO], diag[-HALO:])
    diag = jnp.concatenate([below, diag, above], axis=0)
    place = lax.axis_index(DOM)
    ends = jnp.stack([place == 0, place == lax.axis_size(DOM) - 1]).astype(jnp.int32)
    cells = pltpu.with_memory_space_constraint(
        vectors.reshape(count, planes * rows, lanes), pltpu.MemorySpace.HBM
    )
    ritz_rows = pltpu.with_memory_space_constraint(
        ritz.reshape(-1, *ritz.shape[2:]), pltpu.MemorySpace.HBM
    )
    held, parts = [], []
    for k in range(CHUNKS):
        low, high = spread(cells, rows, k, size)
        low, high = swap_ends(low, high)
        blocks = filtered(ends, cells, low, high, diag, k, size)
        held.append(lax.all_to_all(blocks, VEC, 0, 0, tiled=True))
    column = lax.axis_index(NEAR).reshape(1).astype(jnp.int32)
    for k in range(CHUNKS):
        kind = bf16 if k == CHUNKS - 1 else f32
        partial = projected(held[k], ritz_rows, lax.axis_size(NEAR), column, kind)
        parts.append(near_sum(partial))
    mine, other = summed(parts)
    core = lax.axis_index("c").reshape(1).astype(jnp.int32)
    out = residual(core, mine, other, ritz_rows, held)
    return out.reshape(-1, *coefficient.shape)


def solution(mesh):
    fine = Mesh(mesh.devices.reshape(2, 4, 2, 4, 4), ("zh", "x", "c", "y", "zl"))
    placed = (P(VEC, DOM, None, None), P(DOM, VEC, None), P(DOM, VEC, None, None))
    return jax.shard_map(
        pipeline, mesh=fine, in_specs=placed, out_specs=P(None, DOM, VEC, None), check_vma=False
    )
```

```python
import functools

import jax
import jax.numpy as jnp
from jax import lax
from jax.experimental import pallas as pl
from jax.experimental.pallas import tpu as pltpu
from jax.sharding import Mesh, PartitionSpec as P

bf16 = jnp.bfloat16
f32 = jnp.float32

VEC = ("zh", "x", "c")
DOM = ("y", "zl")
SHARE = ("y", "x")
NEAR = ("c", *SHARE)
HALO = 4
GROUP = 16
CHUNKS = 2


def spread_kernel(first_ref, second_ref, low_ref, high_ref):
    for source, target in ((first_ref, low_ref), (second_ref, high_ref)):
        vectors, rows, lanes = source.shape
        flat = source.reshape(vectors * rows, lanes)
        for y in range(rows):
            target[0, y] = flat[pl.ds(y, vectors, stride=rows), :].astype(bf16)


def spread(cells, rows, chunk, size):
    planes, lanes = cells.shape[1] // rows, cells.shape[2]
    half = planes // 2
    out = pl.BlockSpec((1, rows, size, lanes), lambda p: (p, 0, 0, 0))
    return pl.pallas_call(
        spread_kernel,
        out_shape=[jax.ShapeDtypeStruct((half, rows, size, lanes), bf16)] * 2,
        grid=(half,),
        in_specs=[
            pl.BlockSpec((size, rows, lanes), lambda p: (chunk, p, 0)),
            pl.BlockSpec((size, rows, lanes), lambda p: (chunk, p + half, 0)),
        ],
        out_specs=[out] * 2,
        compiler_params=pltpu.CompilerParams(vmem_limit_bytes=8 << 20),
        cost_estimate=pl.CostEstimate(
            flops=size * planes * rows * lanes,
            bytes_accessed=6 * size * planes * rows * lanes,
            transcendentals=0,
        ),
    )(cells, cells)


def filter_kernel(ends_ref, own_ref, low_ref, high_ref, diag_ref, out_ref, even, odd):
    total, rows, lanes = diag_ref.shape
    planes = total - 2 * HALO
    flat = own_ref.reshape(GROUP * planes * rows, lanes)
    lane = lax.broadcasted_iota(jnp.int32, (GROUP, lanes), 1)
    first, last = lane == 0, lane == lanes - 1

    def fill(p, carry):
        for y in range(rows):
            even[p, y] = low_ref[p, y].astype(f32)
            even[p + HALO + planes, y] = high_ref[p, y].astype(f32)
        return carry

    lax.fori_loop(0, HALO, fill, 0)

    def copy(p, carry):
        for y in range(rows):
            at = pl.ds(p * rows + y, GROUP, stride=planes * rows)
            even[p + HALO, y] = flat[at, :]
        return carry

    lax.fori_loop(0, planes, copy, 0)

    def step(source, target, weight, reach, scale):
        def plane(p, carry):
            below = None
            here = source[p, 0]
            for y in range(rows):
                above = source[p, y + 1] if y + 1 < rows else None
                left = jnp.where(first, 0.0, pltpu.roll(here, 1, 1))
                right = jnp.where(last, 0.0, pltpu.roll(here, lanes - 1, 1))
                beside = (source[p - 1, y] + source[p + 1, y]) + (left + right)
                if below is not None:
                    beside = beside + below
                if above is not None:
                    beside = beside + above
                value = diag_ref[p, pl.ds(y, 1), :] * here - beside
                if weight:
                    value = value - weight * target[p, y]
                if scale:
                    out_ref[y // 2, 2 * (p - HALO) + y % 2] = (value * scale).astype(bf16)
                else:
                    target[p, y] = value
                below, here = here, above
            return carry

        lax.fori_loop(reach, total - reach, plane, 0)
        if reach < HALO:
            zero = jnp.zeros((GROUP, lanes), f32)

            def clear(at):
                def one(p, carry):
                    for y in range(rows):
                        target[at + p, y] = zero
                    return carry

                lax.fori_loop(0, HALO - reach, one, 0)

            @pl.when(ends_ref[0] == 1)
            def _():
                clear(reach)

            @pl.when(ends_ref[1] == 1)
            def _():
                clear(HALO + planes)

    step(even, odd, 0.0, 1, 0.0)
    step(odd, even, 24.5, 2, 0.0)
    step(even, odd, 12.25, 3, 0.0)
    step(odd, even, 12.25, 4, 8.0 / 2401.0)


def filtered(ends, cells, low, high, diag, chunk, size):
    total, rows, lanes = diag.shape
    planes = total - 2 * HALO
    groups = size // GROUP
    edge = pl.BlockSpec((HALO, rows, GROUP, lanes), lambda g: (0, 0, g, 0))
    return pl.pallas_call(
        filter_kernel,
        out_shape=jax.ShapeDtypeStruct((rows // 2, 2 * planes, size, lanes), bf16),
        grid=(groups,),
        in_specs=[
            pl.BlockSpec(memory_space=pltpu.SMEM),
            pl.BlockSpec((GROUP, planes * rows, lanes), lambda g: (chunk * groups + g, 0, 0)),
            edge,
            edge,
            pl.BlockSpec((total, rows, lanes), lambda g: (0, 0, 0)),
        ],
        out_specs=pl.BlockSpec((rows // 2, 2 * planes, GROUP, lanes), lambda g: (0, 0, g, 0)),
        scratch_shapes=[pltpu.VMEM((total, rows, GROUP, lanes), f32)] * 2,
        compiler_params=pltpu.CompilerParams(vmem_limit_bytes=24 << 20),
        cost_estimate=pl.CostEstimate(
            flops=12 * 44 * rows * size * lanes, bytes_accessed=5 << 20, transcendentals=0
        ),
    )(ends, cells, low, high, diag)


def project_kernel(place_ref, ritz_ref, cells_ref, out_ref, *refs):
    *kept_refs, total = refs
    step = pl.program_id(0)
    lanes = cells_ref.shape[3]

    @pl.when(step == 0)
    def _():
        total[...] = jnp.zeros_like(total)

    pair = jnp.concatenate(
        [cells_ref[:, 0].reshape(-1, lanes), cells_ref[:, 1].reshape(-1, lanes)], axis=1
    )
    total[...] += jnp.dot(
        pair, ritz_ref[...].reshape(2 * lanes, -1), preferred_element_type=f32
    )
    for kept_ref in kept_refs:
        kept_ref[pl.ds(2 * step, 2)] = ritz_ref[...]

    @pl.when(step == pl.num_programs(0) - 1)
    def _():
        near, size, _ = out_ref.shape
        if out_ref.dtype == f32:
            for q in range(near):
                out_ref[place_ref[0] ^ q] = total[q * size : (q + 1) * size, :]
        else:
            out_ref[...] = total[...].astype(bf16).reshape(out_ref.shape)


def projected(cells, ritz, near, place, kind):
    blocks, rows, vectors, lanes = cells.shape
    kept = ritz.shape[2]
    count = blocks * vectors
    out_shape = [jax.ShapeDtypeStruct((near, count // near, kept), kind)]
    out_specs = [pl.BlockSpec((near, count // near, kept), lambda r: (0, 0, 0))]
    if kind == bf16:
        out_shape.append(pltpu.VMEM(ritz.shape, ritz.dtype))
        out_specs.append(pl.BlockSpec(memory_space=pltpu.VMEM))
    return pl.pallas_call(
        project_kernel,
        out_shape=out_shape,
        grid=(rows // 2,),
        in_specs=[
            pl.BlockSpec(memory_space=pltpu.SMEM),
            pl.BlockSpec((2, lanes, kept), lambda r: (r, 0, 0)),
            pl.BlockSpec((blocks, 2, vectors, lanes), lambda r: (0, r, 0, 0)),
        ],
        out_specs=out_specs,
        scratch_shapes=[pltpu.VMEM((count, kept), f32)],
        compiler_params=pltpu.CompilerParams(vmem_limit_bytes=24 << 20),
        cost_estimate=pl.CostEstimate(
            flops=2 * count * rows * lanes * kept, bytes_accessed=7 << 20, transcendentals=0
        ),
    )(place, ritz, cells)


def remove_kernel(core_ref, mine_ref, other_ref, ritz_ref, *refs):
    out_ref = refs[-1]
    blocks, rows, vectors, lanes = refs[0].shape
    mine = mine_ref[...].reshape(blocks * vectors // 2, -1)
    other = other_ref[...].reshape(blocks * vectors // 2, -1)
    first = core_ref[0] == 0
    coeffs = jnp.concatenate(
        [jnp.where(first, mine, other), jnp.where(first, other, mine)], axis=0
    )

    def remove(cells_ref):
        for r in range(0, rows, 2):
            removed = lax.dot_general(
                coeffs,
                ritz_ref[r : r + 2].reshape(2 * lanes, -1),
                (((1,), (1,)), ((), ())),
                preferred_element_type=f32,
            )
            for k in range(2):
                for i in range(blocks):
                    held = cells_ref[i, r + k].astype(f32)
                    part = removed[i * vectors : (i + 1) * vectors, k * lanes : (k + 1) * lanes]
                    out_ref[i, pl.ds(r + k, vectors, stride=rows), :] = held - part

    for k, cells_ref in enumerate(refs[:-1]):
        pl.when(pl.program_id(0) == k)(functools.partial(remove, cells_ref))


def residual(core, mine, other, ritz, held):
    blocks, rows, vectors, lanes = held[0].shape
    near, _, kept = mine.shape
    chunks = len(held)
    size = mine.shape[1] // chunks
    coeffs = pl.BlockSpec((near, size, kept), lambda k: (0, k, 0))
    return pl.pallas_call(
        remove_kernel,
        out_shape=jax.ShapeDtypeStruct((blocks, chunks * vectors * rows, lanes), f32),
        grid=(chunks,),
        in_specs=[
            pl.BlockSpec(memory_space=pltpu.SMEM),
            coeffs,
            coeffs,
            pl.BlockSpec(memory_space=pltpu.VMEM),
            *([pl.BlockSpec((blocks, rows, vectors, lanes), lambda k: (0, 0, 0, 0))] * chunks),
        ],
        out_specs=pl.BlockSpec((blocks, vectors * rows, lanes), lambda k: (0, k, 0)),
        compiler_params=pltpu.CompilerParams(vmem_limit_bytes=32 << 20),
        cost_estimate=pl.CostEstimate(
            flops=2 * chunks * blocks * vectors * rows * lanes * kept,
            bytes_accessed=11 << 20,
            transcendentals=0,
        ),
    )(core, mine, other, ritz, *held)


def total_of(terms):
    while len(terms) > 1:
        terms = [a + b for a, b in zip(terms[::2], terms[1::2])]
    return terms[0]


def traded(blocks, axis):
    count = lax.axis_size(axis)
    return total_of(
        [blocks[0]]
        + [
            lax.ppermute(blocks[k], axis, [(i, i ^ k) for i in range(count)])
            for k in range(1, count)
        ]
    )


def near_sum(partial):
    if partial.dtype == bf16:
        blocks = lax.all_to_all(partial, NEAR, 0, 0, tiled=True)
        return jnp.sum(blocks.astype(f32), axis=0)
    for axis in NEAR:
        count = lax.axis_size(axis)
        partial = traded(partial.reshape(count, -1, *partial.shape[-2:]), axis)
    return partial[0]


def summed(parts):
    blocks = jnp.concatenate(parts, axis=0)
    blocks = blocks + swapped(blocks, "zh")
    blocks = traded([blocks] * lax.axis_size("zl"), "zl").astype(bf16)
    mine = from_everyone(blocks, SHARE)
    return mine, swapped(mine, "c")


def swapped(value, axis):
    return lax.ppermute(value, axis, [(0, 1), (1, 0)])


def from_everyone(value, axis):
    copies = jnp.broadcast_to(value, (lax.axis_size(axis), *value.shape))
    return lax.all_to_all(copies, axis, split_axis=0, concat_axis=0, tiled=True)


def swap_ends(low, high):
    count = lax.axis_size(DOM)
    from_below = lax.ppermute(high, DOM, [(i, i + 1) for i in range(count - 1)])
    from_above = lax.ppermute(low, DOM, [(i + 1, i) for i in range(count - 1)])
    return from_below, from_above


def pipeline(vectors, coefficient, ritz):
    count, planes, rows, lanes = vectors.shape
    size = count // CHUNKS
    other = swapped(coefficient, "zh")
    first = lax.axis_index("zh") == 0
    diag = jnp.stack(
        [jnp.where(first, coefficient, other), jnp.where(first, other, coefficient)]
    )
    diag = from_everyone(diag, ("x", "c"))
    diag = diag.transpose(2, 1, 0, 3, 4).reshape(planes, rows, lanes) + (6.0 - 7.125)
    below, above = swap_ends(diag[:HALO], diag[-HALO:])
    diag = jnp.concatenate([below, diag, above], axis=0)
    place = lax.axis_index(DOM)
    ends = jnp.stack([place == 0, place == lax.axis_size(DOM) - 1]).astype(jnp.int32)
    cells = pltpu.with_memory_space_constraint(
        vectors.reshape(count, planes * rows, lanes), pltpu.MemorySpace.HBM
    )
    ritz_rows = pltpu.with_memory_space_constraint(
        ritz.reshape(-1, *ritz.shape[2:]), pltpu.MemorySpace.HBM
    )
    held, parts = [], []
    for k in range(CHUNKS):
        low, high = spread(cells, rows, k, size)
        low, high = swap_ends(low, high)
        blocks = filtered(ends, cells, low, high, diag, k, size)
        held.append(lax.all_to_all(blocks, VEC, 0, 0, tiled=True))
    column = lax.axis_index(NEAR).reshape(1).astype(jnp.int32)
    for k in range(CHUNKS):
        kind = bf16 if k == CHUNKS - 1 else f32
        partial, *kept = projected(held[k], ritz_rows, lax.axis_size(NEAR), column, kind)
        if parts:
            partial, parts[-1] = lax.optimization_barrier((partial, parts[-1]))
        parts.append(near_sum(partial))
    mine, other = summed(parts)
    core = lax.axis_index("c").reshape(1).astype(jnp.int32)
    out = residual(core, mine, other, kept[0], held)
    return out.reshape(-1, *coefficient.shape)


def solution(mesh):
    fine = Mesh(mesh.devices.reshape(2, 4, 2, 4, 4), ("zh", "x", "c", "y", "zl"))
    placed = (P(VEC, DOM, None, None), P(DOM, VEC, None), P(DOM, VEC, None, None))
    return jax.shard_map(
        pipeline, mesh=fine, in_specs=placed, out_specs=P(None, DOM, VEC, None), check_vma=False
    )
```

```python
import functools

import jax
import jax.numpy as jnp
from jax import lax
from jax.experimental import pallas as pl
from jax.experimental.pallas import tpu as pltpu
from jax.sharding import Mesh, PartitionSpec as P

bf16 = jnp.bfloat16
f32 = jnp.float32

VEC = ("zh", "x", "c")
DOM = ("y", "zl")
SHARE = ("y", "x")
NEAR = ("c", *SHARE)
HALO = 4
GROUP = 16
CHUNKS = 2


def spread_kernel(first_ref, second_ref, low_ref, high_ref):
    for source, target in ((first_ref, low_ref), (second_ref, high_ref)):
        vectors, rows, lanes = source.shape
        flat = source.reshape(vectors * rows, lanes)
        for y in range(rows):
            target[0, y] = flat[pl.ds(y, vectors, stride=rows), :].astype(bf16)


def spread(cells, rows, chunk, size):
    planes, lanes = cells.shape[1] // rows, cells.shape[2]
    half = planes // 2
    out = pl.BlockSpec((1, rows, size, lanes), lambda p: (p, 0, 0, 0))
    return pl.pallas_call(
        spread_kernel,
        out_shape=[jax.ShapeDtypeStruct((half, rows, size, lanes), bf16)] * 2,
        grid=(half,),
        in_specs=[
            pl.BlockSpec((size, rows, lanes), lambda p: (chunk, p, 0)),
            pl.BlockSpec((size, rows, lanes), lambda p: (chunk, p + half, 0)),
        ],
        out_specs=[out] * 2,
        compiler_params=pltpu.CompilerParams(vmem_limit_bytes=8 << 20),
        cost_estimate=pl.CostEstimate(
            flops=size * planes * rows * lanes,
            bytes_accessed=6 * size * planes * rows * lanes,
            transcendentals=0,
        ),
    )(cells, cells)


def filter_kernel(ends_ref, own_ref, low_ref, high_ref, diag_ref, out_ref, even, odd):
    total, rows, lanes = diag_ref.shape
    planes = total - 2 * HALO
    flat = own_ref.reshape(GROUP * planes * rows, lanes)
    lane = lax.broadcasted_iota(jnp.int32, (GROUP, lanes), 1)
    first, last = lane == 0, lane == lanes - 1

    def fill(p, carry):
        for y in range(rows):
            even[p, y] = low_ref[p, y].astype(f32)
            even[p + HALO + planes, y] = high_ref[p, y].astype(f32)
        return carry

    lax.fori_loop(0, HALO, fill, 0)

    def copy(p, carry):
        for y in range(rows):
            at = pl.ds(p * rows + y, GROUP, stride=planes * rows)
            even[p + HALO, y] = flat[at, :]
        return carry

    lax.fori_loop(0, planes, copy, 0)

    def step(source, target, weight, reach, scale):
        def plane(p, carry):
            below = None
            here = source[p, 0]
            for y in range(rows):
                above = source[p, y + 1] if y + 1 < rows else None
                left = jnp.where(first, 0.0, pltpu.roll(here, 1, 1))
                right = jnp.where(last, 0.0, pltpu.roll(here, lanes - 1, 1))
                beside = (source[p - 1, y] + source[p + 1, y]) + (left + right)
                if below is not None:
                    beside = beside + below
                if above is not None:
                    beside = beside + above
                value = diag_ref[p, pl.ds(y, 1), :] * here - beside
                if weight:
                    value = value - weight * target[p, y]
                if scale:
                    out_ref[y // 2, 2 * (p - HALO) + y % 2] = (value * scale).astype(bf16)
                else:
                    target[p, y] = value
                below, here = here, above
            return carry

        lax.fori_loop(reach, total - reach, plane, 0)
        if reach < HALO:
            zero = jnp.zeros((GROUP, lanes), f32)

            def clear(at):
                def one(p, carry):
                    for y in range(rows):
                        target[at + p, y] = zero
                    return carry

                lax.fori_loop(0, HALO - reach, one, 0)

            @pl.when(ends_ref[0] == 1)
            def _():
                clear(reach)

            @pl.when(ends_ref[1] == 1)
            def _():
                clear(HALO + planes)

    step(even, odd, 0.0, 1, 0.0)
    step(odd, even, 24.5, 2, 0.0)
    step(even, odd, 12.25, 3, 0.0)
    step(odd, even, 12.25, 4, 8.0 / 2401.0)


def split_filter_kernel(ends_ref, own_ref, low_ref, high_ref, diag_ref, *refs):
    *out_refs, packed_ref, even, odd, blocks, sems = refs
    filter_kernel(ends_ref, own_ref, low_ref, high_ref, diag_ref, blocks, even, odd)
    half = len(out_refs)
    copies = []
    for k, out_ref in enumerate(out_refs):
        copies.append(pltpu.make_async_copy(blocks.at[ends_ref[2] ^ k], out_ref, sems.at[k]))
        copies.append(
            pltpu.make_async_copy(
                blocks.at[ends_ref[2] ^ (half + k)], packed_ref.at[k], sems.at[half + k]
            )
        )
    for copy in copies:
        copy.start()
    for copy in copies:
        copy.wait()


def filtered(ends, cells, low, high, diag, chunk, size, split):
    total, rows, lanes = diag.shape
    planes = total - 2 * HALO
    groups = size // GROUP
    edge = pl.BlockSpec((HALO, rows, GROUP, lanes), lambda g: (0, 0, g, 0))
    count, shape = rows // 2, (2 * planes, GROUP, lanes)
    scratch = [pltpu.VMEM((total, rows, GROUP, lanes), f32)] * 2
    if split:
        half = count // 2
        out_shape = [jax.ShapeDtypeStruct(shape, bf16)] * half
        out_shape.append(jax.ShapeDtypeStruct((half, *shape), bf16))
        out_specs = [pl.BlockSpec(memory_space=pl.ANY)] * (half + 1)
        scratch += [pltpu.VMEM((count, *shape), bf16), pltpu.SemaphoreType.DMA((count,))]
    else:
        out_shape = jax.ShapeDtypeStruct((count, 2 * planes, size, lanes), bf16)
        out_specs = pl.BlockSpec((count, *shape), lambda g: (0, 0, g, 0))
    return pl.pallas_call(
        split_filter_kernel if split else filter_kernel,
        out_shape=out_shape,
        grid=(groups,),
        in_specs=[
            pl.BlockSpec(memory_space=pltpu.SMEM),
            pl.BlockSpec((GROUP, planes * rows, lanes), lambda g: (chunk * groups + g, 0, 0)),
            edge,
            edge,
            pl.BlockSpec((total, rows, lanes), lambda g: (0, 0, 0)),
        ],
        out_specs=out_specs,
        scratch_shapes=scratch,
        compiler_params=pltpu.CompilerParams(vmem_limit_bytes=24 << 20),
        cost_estimate=pl.CostEstimate(
            flops=12 * 44 * rows * size * lanes, bytes_accessed=5 << 20, transcendentals=0
        ),
    )(ends, cells, low, high, diag)


def project_kernel(ritz_ref, cells_ref, out_ref, kept_ref, total):
    step = pl.program_id(0)
    lanes = cells_ref.shape[3]
    pair = jnp.concatenate(
        [cells_ref[:, 0].reshape(-1, lanes), cells_ref[:, 1].reshape(-1, lanes)], axis=1
    )
    accumulate(pair, ritz_ref, total)
    kept_ref[pl.ds(2 * step, 2)] = ritz_ref[...]

    @pl.when(step == pl.num_programs(0) - 1)
    def _():
        out_ref[...] = total[...].astype(bf16).reshape(out_ref.shape)


def accumulate(pair, ritz_ref, total):
    @pl.when(pl.program_id(0) == 0)
    def _():
        total[...] = jnp.zeros_like(total)

    total[...] += jnp.dot(
        pair, ritz_ref[...].reshape(pair.shape[1], -1), preferred_element_type=f32
    )


def joined_project_kernel(place_ref, ritz_ref, *refs):
    *block_refs, out_ref, held_ref, total, pairs = refs
    for k, block_ref in enumerate(block_refs):
        source = place_ref[1] ^ k
        held_ref[source] = block_ref[...]
        pairs[source] = jnp.concatenate([block_ref[0], block_ref[1]], axis=1)
    accumulate(pairs[...].reshape(-1, pairs.shape[2]), ritz_ref, total)

    @pl.when(pl.program_id(0) == pl.num_programs(0) - 1)
    def _():
        near, size, _ = out_ref.shape
        for q in range(near):
            out_ref[place_ref[0] ^ q] = total[q * size : (q + 1) * size, :]


def projected(cells, ritz, near, place):
    joined = isinstance(cells, list)
    blocks = len(cells)
    rows, vectors, lanes = cells[0].shape
    kept = ritz.shape[2]
    count = blocks * vectors
    block = pl.BlockSpec((blocks, 2, vectors, lanes), lambda r: (0, r, 0, 0))
    rhs = pl.BlockSpec((2, lanes, kept), lambda r: (r, 0, 0))
    scratch = [pltpu.VMEM((count, kept), f32)]
    if joined:
        operands = [place, ritz, *cells]
        in_specs = [pl.BlockSpec(memory_space=pltpu.SMEM), rhs]
        in_specs += [pl.BlockSpec((2, vectors, lanes), lambda r: (r, 0, 0))] * blocks
        second = jax.ShapeDtypeStruct((blocks, rows, vectors, lanes), bf16)
        second_spec = block
        scratch.append(pltpu.VMEM((blocks, vectors, 2 * lanes), bf16))
    else:
        operands = [ritz, cells]
        in_specs = [rhs, block]
        second = pltpu.VMEM(ritz.shape, ritz.dtype)
        second_spec = pl.BlockSpec(memory_space=pltpu.VMEM)
    return pl.pallas_call(
        joined_project_kernel if joined else project_kernel,
        out_shape=[
            jax.ShapeDtypeStruct((near, count // near, kept), f32 if joined else bf16),
            second,
        ],
        grid=(rows // 2,),
        in_specs=in_specs,
        out_specs=[pl.BlockSpec((near, count // near, kept), lambda r: (0, 0, 0)), second_spec],
        scratch_shapes=scratch,
        compiler_params=pltpu.CompilerParams(vmem_limit_bytes=24 << 20),
        cost_estimate=pl.CostEstimate(
            flops=2 * count * rows * lanes * kept, bytes_accessed=7 << 20, transcendentals=0
        ),
    )(*operands)


def remove_kernel(core_ref, mine_ref, other_ref, ritz_ref, *refs):
    out_ref = refs[-1]
    blocks, rows, vectors, lanes = refs[0].shape
    mine = mine_ref[...].reshape(blocks * vectors // 2, -1)
    other = other_ref[...].reshape(blocks * vectors // 2, -1)
    first = core_ref[0] == 0
    coeffs = jnp.concatenate(
        [jnp.where(first, mine, other), jnp.where(first, other, mine)], axis=0
    )

    def remove(cells_ref):
        for r in range(0, rows, 2):
            removed = lax.dot_general(
                coeffs,
                ritz_ref[r : r + 2].reshape(2 * lanes, -1),
                (((1,), (1,)), ((), ())),
                preferred_element_type=f32,
            )
            for k in range(2):
                for i in range(blocks):
                    held = cells_ref[i, r + k].astype(f32)
                    part = removed[i * vectors : (i + 1) * vectors, k * lanes : (k + 1) * lanes]
                    out_ref[i, pl.ds(r + k, vectors, stride=rows), :] = held - part

    for k, cells_ref in enumerate(refs[:-1]):
        pl.when(pl.program_id(0) == k)(functools.partial(remove, cells_ref))


def residual(core, mine, other, ritz, held):
    blocks, rows, vectors, lanes = held[0].shape
    near, _, kept = mine.shape
    chunks = len(held)
    size = mine.shape[1] // chunks
    coeffs = pl.BlockSpec((near, size, kept), lambda k: (0, k, 0))
    return pl.pallas_call(
        remove_kernel,
        out_shape=jax.ShapeDtypeStruct((blocks, chunks * vectors * rows, lanes), f32),
        grid=(chunks,),
        in_specs=[
            pl.BlockSpec(memory_space=pltpu.SMEM),
            coeffs,
            coeffs,
            pl.BlockSpec(memory_space=pltpu.VMEM),
            *([pl.BlockSpec((blocks, rows, vectors, lanes), lambda k: (0, 0, 0, 0))] * chunks),
        ],
        out_specs=pl.BlockSpec((blocks, vectors * rows, lanes), lambda k: (0, k, 0)),
        compiler_params=pltpu.CompilerParams(vmem_limit_bytes=32 << 20),
        cost_estimate=pl.CostEstimate(
            flops=2 * chunks * blocks * vectors * rows * lanes * kept,
            bytes_accessed=11 << 20,
            transcendentals=0,
        ),
    )(core, mine, other, ritz, *held)


def total_of(terms):
    while len(terms) > 1:
        terms = [a + b for a, b in zip(terms[::2], terms[1::2])]
    return terms[0]


def traded(blocks, axis):
    count = lax.axis_size(axis)
    return total_of(
        [blocks[0]]
        + [
            lax.ppermute(blocks[k], axis, [(i, i ^ k) for i in range(count)])
            for k in range(1, count)
        ]
    )


def exchanged(blocks):
    *own, packed = blocks
    local = ("x", "c")
    size = lax.axis_size(local)

    def passed_on(pieces):
        return [pieces[0]] + [
            lax.ppermute(pieces[d], local, [(i, i ^ d) for i in range(size)])
            for d in range(1, size)
        ]

    packed = swapped(packed, "zh")
    own = passed_on(own)
    rest = passed_on([packed[d] for d in range(size)])
    return own + rest


def near_sum(partial):
    if partial.dtype == bf16:
        blocks = lax.all_to_all(partial, NEAR, 0, 0, tiled=True)
        return jnp.sum(blocks.astype(f32), axis=0)
    for axis in NEAR:
        count = lax.axis_size(axis)
        partial = traded(partial.reshape(count, -1, *partial.shape[-2:]), axis)
    return partial[0]


def summed(parts):
    blocks = jnp.concatenate(parts, axis=0)
    blocks = blocks + swapped(blocks, "zh")
    blocks = traded([blocks] * lax.axis_size("zl"), "zl").astype(bf16)
    mine = from_everyone(blocks, SHARE)
    return mine, swapped(mine, "c")


def swapped(value, axis):
    return lax.ppermute(value, axis, [(0, 1), (1, 0)])


def from_everyone(value, axis):
    copies = jnp.broadcast_to(value, (lax.axis_size(axis), *value.shape))
    return lax.all_to_all(copies, axis, split_axis=0, concat_axis=0, tiled=True)


def swap_ends(low, high):
    count = lax.axis_size(DOM)
    from_below = lax.ppermute(high, DOM, [(i, i + 1) for i in range(count - 1)])
    from_above = lax.ppermute(low, DOM, [(i + 1, i) for i in range(count - 1)])
    return from_below, from_above


def pipeline(vectors, coefficient, ritz):
    count, planes, rows, lanes = vectors.shape
    size = count // CHUNKS
    other = swapped(coefficient, "zh")
    first = lax.axis_index("zh") == 0
    diag = jnp.stack(
        [jnp.where(first, coefficient, other), jnp.where(first, other, coefficient)]
    )
    diag = from_everyone(diag, ("x", "c"))
    diag = diag.transpose(2, 1, 0, 3, 4).reshape(planes, rows, lanes) + (6.0 - 7.125)
    below, above = swap_ends(diag[:HALO], diag[-HALO:])
    diag = jnp.concatenate([below, diag, above], axis=0)
    place = lax.axis_index(DOM)
    ends = jnp.stack([place == 0, place == lax.axis_size(DOM) - 1]).astype(jnp.int32)
    ends = jnp.concatenate([ends, lax.axis_index(VEC).reshape(1).astype(jnp.int32)])
    cells = pltpu.with_memory_space_constraint(
        vectors.reshape(count, planes * rows, lanes), pltpu.MemorySpace.HBM
    )
    ritz_rows = pltpu.with_memory_space_constraint(
        ritz.reshape(-1, *ritz.shape[2:]), pltpu.MemorySpace.HBM
    )
    held, parts = [], []
    for k in range(CHUNKS):
        split = k < CHUNKS - 1
        low, high = spread(cells, rows, k, size)
        low, high = swap_ends(low, high)
        blocks = filtered(ends, cells, low, high, diag, k, size, split)
        if split:
            held.append(exchanged(blocks))
        else:
            held.append(lax.all_to_all(blocks, VEC, 0, 0, tiled=True))
    places = jnp.stack([lax.axis_index(NEAR), lax.axis_index(VEC)]).astype(jnp.int32)
    for k in range(CHUNKS):
        partial, second = projected(held[k], ritz_rows, lax.axis_size(NEAR), places)
        if isinstance(held[k], list):
            held[k] = second
        else:
            kept = second
        if parts:
            partial, parts[-1] = lax.optimization_barrier((partial, parts[-1]))
        parts.append(near_sum(partial))
    mine, other = summed(parts)
    core = lax.axis_index("c").reshape(1).astype(jnp.int32)
    out = residual(core, mine, other, kept, held)
    return out.reshape(-1, *coefficient.shape)


def solution(mesh):
    fine = Mesh(mesh.devices.reshape(2, 4, 2, 4, 4), ("zh", "x", "c", "y", "zl"))
    placed = (P(VEC, DOM, None, None), P(DOM, VEC, None), P(DOM, VEC, None, None))
    return jax.shard_map(
        pipeline, mesh=fine, in_specs=placed, out_specs=P(None, DOM, VEC, None), check_vma=False
    )
```

```python
import functools

import jax
import jax.numpy as jnp
from jax import lax
from jax.experimental import pallas as pl
from jax.experimental.pallas import tpu as pltpu
from jax.sharding import Mesh, PartitionSpec as P

bf16 = jnp.bfloat16
f32 = jnp.float32

VEC = ("zh", "x", "c")
DOM = ("y", "zl")
SHARE = ("y", "x")
NEAR = ("c", *SHARE)
HALO = 4
GROUP = 16
CHUNKS = 2
STEP = 4


def spread_kernel(first_ref, second_ref, low_ref, high_ref):
    for source, target in ((first_ref, low_ref), (second_ref, high_ref)):
        vectors, rows, lanes = source.shape
        flat = source.reshape(vectors * rows, lanes)
        for y in range(rows):
            target[0, y] = flat[pl.ds(y, vectors, stride=rows), :].astype(bf16)


def spread(cells, rows, chunk, size):
    planes, lanes = cells.shape[1] // rows, cells.shape[2]
    half = planes // 2
    out = pl.BlockSpec((1, rows, size, lanes), lambda p: (p, 0, 0, 0))
    return pl.pallas_call(
        spread_kernel,
        out_shape=[jax.ShapeDtypeStruct((half, rows, size, lanes), bf16)] * 2,
        grid=(half,),
        in_specs=[
            pl.BlockSpec((size, rows, lanes), lambda p: (chunk, p, 0)),
            pl.BlockSpec((size, rows, lanes), lambda p: (chunk, p + half, 0)),
        ],
        out_specs=[out] * 2,
        compiler_params=pltpu.CompilerParams(vmem_limit_bytes=8 << 20),
        cost_estimate=pl.CostEstimate(
            flops=size * planes * rows * lanes,
            bytes_accessed=6 * size * planes * rows * lanes,
            transcendentals=0,
        ),
    )(cells, cells)


def filter_kernel(ends_ref, own_ref, low_ref, high_ref, diag_ref, out_ref, even, odd):
    total, rows, lanes = diag_ref.shape
    planes = total - 2 * HALO
    flat = own_ref.reshape(GROUP * planes * rows, lanes)
    lane = lax.broadcasted_iota(jnp.int32, (GROUP, lanes), 1)
    first, last = lane == 0, lane == lanes - 1

    def fill(p, carry):
        for y in range(rows):
            even[p, y] = low_ref[p, y].astype(f32)
            even[p + HALO + planes, y] = high_ref[p, y].astype(f32)
        return carry

    lax.fori_loop(0, HALO, fill, 0)

    def copy(p, carry):
        for y in range(rows):
            at = pl.ds(p * rows + y, GROUP, stride=planes * rows)
            even[p + HALO, y] = flat[at, :]
        return carry

    lax.fori_loop(0, planes, copy, 0)

    def step(source, target, weight, reach, scale):
        def plane(p, carry):
            below = None
            here = source[p, 0]
            for y in range(rows):
                above = source[p, y + 1] if y + 1 < rows else None
                left = jnp.where(first, 0.0, pltpu.roll(here, 1, 1))
                right = jnp.where(last, 0.0, pltpu.roll(here, lanes - 1, 1))
                beside = (source[p - 1, y] + source[p + 1, y]) + (left + right)
                if below is not None:
                    beside = beside + below
                if above is not None:
                    beside = beside + above
                value = diag_ref[p, pl.ds(y, 1), :] * here - beside
                if weight:
                    value = value - weight * target[p, y]
                if scale:
                    out_ref[y // 2, 2 * (p - HALO) + y % 2] = (value * scale).astype(bf16)
                else:
                    target[p, y] = value
                below, here = here, above
            return carry

        lax.fori_loop(reach, total - reach, plane, 0)
        if reach < HALO:
            zero = jnp.zeros((GROUP, lanes), f32)

            def clear(at):
                def one(p, carry):
                    for y in range(rows):
                        target[at + p, y] = zero
                    return carry

                lax.fori_loop(0, HALO - reach, one, 0)

            @pl.when(ends_ref[0] == 1)
            def _():
                clear(reach)

            @pl.when(ends_ref[1] == 1)
            def _():
                clear(HALO + planes)

    step(even, odd, 0.0, 1, 0.0)
    step(odd, even, 24.5, 2, 0.0)
    step(even, odd, 12.25, 3, 0.0)
    step(odd, even, 12.25, 4, 8.0 / 2401.0)


def filtered(ends, cells, low, high, diag, chunk, size):
    total, rows, lanes = diag.shape
    planes = total - 2 * HALO
    groups = size // GROUP
    edge = pl.BlockSpec((HALO, rows, GROUP, lanes), lambda g: (0, 0, g, 0))
    return pl.pallas_call(
        filter_kernel,
        out_shape=jax.ShapeDtypeStruct((rows // 2, 2 * planes, size, lanes), bf16),
        grid=(groups,),
        in_specs=[
            pl.BlockSpec(memory_space=pltpu.SMEM),
            pl.BlockSpec((GROUP, planes * rows, lanes), lambda g: (chunk * groups + g, 0, 0)),
            edge,
            edge,
            pl.BlockSpec((total, rows, lanes), lambda g: (0, 0, 0)),
        ],
        out_specs=pl.BlockSpec((rows // 2, 2 * planes, GROUP, lanes), lambda g: (0, 0, g, 0)),
        scratch_shapes=[pltpu.VMEM((total, rows, GROUP, lanes), f32)] * 2,
        compiler_params=pltpu.CompilerParams(vmem_limit_bytes=24 << 20),
        cost_estimate=pl.CostEstimate(
            flops=12 * 44 * rows * size * lanes, bytes_accessed=5 << 20, transcendentals=0
        ),
    )(ends, cells, low, high, diag)


def project_kernel(place_ref, ritz_ref, cells_ref, out_ref, *refs):
    *kept_refs, total = refs
    step = pl.program_id(0)
    lanes = cells_ref.shape[3]

    @pl.when(step == 0)
    def _():
        total[...] = jnp.zeros_like(total)

    part = jnp.concatenate(
        [cells_ref[:, k].reshape(-1, lanes) for k in range(STEP)], axis=1
    )
    total[...] += jnp.dot(
        part, ritz_ref[...].reshape(STEP * lanes, -1), preferred_element_type=f32
    )
    for kept_ref in kept_refs:
        kept_ref[pl.ds(STEP * step, STEP)] = ritz_ref[...]

    @pl.when(step == pl.num_programs(0) - 1)
    def _():
        near, size, _ = out_ref.shape
        if out_ref.dtype == f32:
            for q in range(near):
                out_ref[place_ref[0] ^ q] = total[q * size : (q + 1) * size, :]
        else:
            out_ref[...] = total[...].astype(bf16).reshape(out_ref.shape)


def projected(cells, ritz, near, place, kind):
    blocks, rows, vectors, lanes = cells.shape
    kept = ritz.shape[2]
    count = blocks * vectors
    out_shape = [jax.ShapeDtypeStruct((near, count // near, kept), kind)]
    out_specs = [pl.BlockSpec((near, count // near, kept), lambda r: (0, 0, 0))]
    if kind == bf16:
        out_shape.append(pltpu.VMEM(ritz.shape, ritz.dtype))
        out_specs.append(pl.BlockSpec(memory_space=pltpu.VMEM))
    return pl.pallas_call(
        project_kernel,
        out_shape=out_shape,
        grid=(rows // STEP,),
        in_specs=[
            pl.BlockSpec(memory_space=pltpu.SMEM),
            pl.BlockSpec((STEP, lanes, kept), lambda r: (r, 0, 0)),
            pl.BlockSpec((blocks, STEP, vectors, lanes), lambda r: (0, r, 0, 0)),
        ],
        out_specs=out_specs,
        scratch_shapes=[pltpu.VMEM((count, kept), f32)],
        compiler_params=pltpu.CompilerParams(vmem_limit_bytes=24 << 20),
        cost_estimate=pl.CostEstimate(
            flops=2 * count * rows * lanes * kept, bytes_accessed=7 << 20, transcendentals=0
        ),
    )(place, ritz, cells)


def remove_kernel(core_ref, mine_ref, other_ref, ritz_ref, *refs):
    out_ref = refs[-1]
    blocks, rows, vectors, lanes = refs[0].shape
    mine = mine_ref[...].reshape(blocks * vectors // 2, -1)
    other = other_ref[...].reshape(blocks * vectors // 2, -1)
    first = core_ref[0] == 0
    coeffs = jnp.concatenate(
        [jnp.where(first, mine, other), jnp.where(first, other, mine)], axis=0
    )

    def remove(cells_ref):
        for r in range(0, rows, 2):
            removed = lax.dot_general(
                coeffs,
                ritz_ref[r : r + 2].reshape(2 * lanes, -1),
                (((1,), (1,)), ((), ())),
                preferred_element_type=f32,
            )
            for k in range(2):
                for i in range(blocks):
                    held = cells_ref[i, r + k].astype(f32)
                    part = removed[i * vectors : (i + 1) * vectors, k * lanes : (k + 1) * lanes]
                    out_ref[i, pl.ds(r + k, vectors, stride=rows), :] = held - part

    for k, cells_ref in enumerate(refs[:-1]):
        pl.when(pl.program_id(0) == k)(functools.partial(remove, cells_ref))


def residual(core, mine, other, ritz, held):
    blocks, rows, vectors, lanes = held[0].shape
    near, _, kept = mine.shape
    chunks = len(held)
    size = mine.shape[1] // chunks
    coeffs = pl.BlockSpec((near, size, kept), lambda k: (0, k, 0))
    return pl.pallas_call(
        remove_kernel,
        out_shape=jax.ShapeDtypeStruct((blocks, chunks * vectors * rows, lanes), f32),
        grid=(chunks,),
        in_specs=[
            pl.BlockSpec(memory_space=pltpu.SMEM),
            coeffs,
            coeffs,
            pl.BlockSpec(memory_space=pltpu.VMEM),
            *([pl.BlockSpec((blocks, rows, vectors, lanes), lambda k: (0, 0, 0, 0))] * chunks),
        ],
        out_specs=pl.BlockSpec((blocks, vectors * rows, lanes), lambda k: (0, k, 0)),
        compiler_params=pltpu.CompilerParams(vmem_limit_bytes=32 << 20),
        cost_estimate=pl.CostEstimate(
            flops=2 * chunks * blocks * vectors * rows * lanes * kept,
            bytes_accessed=11 << 20,
            transcendentals=0,
        ),
    )(core, mine, other, ritz, *held)


def total_of(terms):
    while len(terms) > 1:
        terms = [a + b for a, b in zip(terms[::2], terms[1::2])]
    return terms[0]


def traded(blocks, axis):
    count = lax.axis_size(axis)
    return total_of(
        [blocks[0]]
        + [
            lax.ppermute(blocks[k], axis, [(i, i ^ k) for i in range(count)])
            for k in range(1, count)
        ]
    )


def near_sum(partial):
    if partial.dtype == bf16:
        blocks = lax.all_to_all(partial, NEAR, 0, 0, tiled=True)
        return jnp.sum(blocks.astype(f32), axis=0)
    for axis in NEAR:
        count = lax.axis_size(axis)
        partial = traded(partial.reshape(count, -1, *partial.shape[-2:]), axis)
    return partial[0]


def summed(parts):
    blocks = jnp.concatenate(parts, axis=0)
    blocks = blocks + swapped(blocks, "zh")
    blocks = traded([blocks] * lax.axis_size("zl"), "zl").astype(bf16)
    mine = from_everyone(blocks, SHARE)
    return mine, swapped(mine, "c")


def swapped(value, axis):
    return lax.ppermute(value, axis, [(0, 1), (1, 0)])


def from_everyone(value, axis):
    copies = jnp.broadcast_to(value, (lax.axis_size(axis), *value.shape))
    return lax.all_to_all(copies, axis, split_axis=0, concat_axis=0, tiled=True)


def swap_ends(low, high):
    count = lax.axis_size(DOM)
    from_below = lax.ppermute(high, DOM, [(i, i + 1) for i in range(count - 1)])
    from_above = lax.ppermute(low, DOM, [(i + 1, i) for i in range(count - 1)])
    return from_below, from_above


def pipeline(vectors, coefficient, ritz):
    count, planes, rows, lanes = vectors.shape
    size = count // CHUNKS
    other = swapped(coefficient, "zh")
    first = lax.axis_index("zh") == 0
    diag = jnp.stack(
        [jnp.where(first, coefficient, other), jnp.where(first, other, coefficient)]
    )
    diag = from_everyone(diag, ("x", "c"))
    diag = diag.transpose(2, 1, 0, 3, 4).reshape(planes, rows, lanes) + (6.0 - 7.125)
    below, above = swap_ends(diag[:HALO], diag[-HALO:])
    diag = jnp.concatenate([below, diag, above], axis=0)
    place = lax.axis_index(DOM)
    ends = jnp.stack([place == 0, place == lax.axis_size(DOM) - 1]).astype(jnp.int32)
    cells = pltpu.with_memory_space_constraint(
        vectors.reshape(count, planes * rows, lanes), pltpu.MemorySpace.HBM
    )
    ritz_rows = pltpu.with_memory_space_constraint(
        ritz.reshape(-1, *ritz.shape[2:]), pltpu.MemorySpace.HBM
    )
    held, parts = [], []
    for k in range(CHUNKS):
        low, high = spread(cells, rows, k, size)
        low, high = swap_ends(low, high)
        blocks = filtered(ends, cells, low, high, diag, k, size)
        held.append(lax.all_to_all(blocks, VEC, 0, 0, tiled=True))
    column = lax.axis_index(NEAR).reshape(1).astype(jnp.int32)
    for k in range(CHUNKS):
        kind = bf16 if k == CHUNKS - 1 else f32
        partial, *kept = projected(held[k], ritz_rows, lax.axis_size(NEAR), column, kind)
        if parts:
            partial, parts[-1] = lax.optimization_barrier((partial, parts[-1]))
        parts.append(near_sum(partial))
    mine, other = summed(parts)
    core = lax.axis_index("c").reshape(1).astype(jnp.int32)
    out = residual(core, mine, other, kept[0], held)
    return out.reshape(-1, *coefficient.shape)


def solution(mesh):
    fine = Mesh(mesh.devices.reshape(2, 4, 2, 4, 4), ("zh", "x", "c", "y", "zl"))
    placed = (P(VEC, DOM, None, None), P(DOM, VEC, None), P(DOM, VEC, None, None))
    return jax.shard_map(
        pipeline, mesh=fine, in_specs=placed, out_specs=P(None, DOM, VEC, None), check_vma=False
    )
```

```python
import functools

import jax
import jax.numpy as jnp
from jax import lax
from jax.experimental import pallas as pl
from jax.experimental.pallas import tpu as pltpu
from jax.sharding import Mesh, PartitionSpec as P

bf16 = jnp.bfloat16
f32 = jnp.float32

VEC = ("zh", "x", "c")
DOM = ("y", "zl")
SHARE = ("y", "x")
NEAR = ("c", *SHARE)
HALO = 4
GROUP = 16
CHUNKS = 2
STEP = 4


def spread_kernel(first_ref, second_ref, low_ref, high_ref):
    for source, target in ((first_ref, low_ref), (second_ref, high_ref)):
        planes, rows = target.shape[:2]
        vectors, span, lanes = source.shape
        flat = source.reshape(vectors * span, lanes)
        for p in range(planes):
            for y in range(rows):
                at = pl.ds(p * rows + y, vectors, stride=span)
                target[p, y] = flat[at, :].astype(bf16)


def spread(cells, rows, chunk, size):
    planes, lanes = cells.shape[1] // rows, cells.shape[2]
    half = planes // 2
    steps = half // 2
    out = pl.BlockSpec((2, rows, size, lanes), lambda p: (p, 0, 0, 0))
    return pl.pallas_call(
        spread_kernel,
        out_shape=[jax.ShapeDtypeStruct((half, rows, size, lanes), bf16)] * 2,
        grid=(steps,),
        in_specs=[
            pl.BlockSpec((size, 2 * rows, lanes), lambda p: (chunk, p, 0)),
            pl.BlockSpec((size, 2 * rows, lanes), lambda p: (chunk, p + steps, 0)),
        ],
        out_specs=[out] * 2,
        compiler_params=pltpu.CompilerParams(vmem_limit_bytes=10 << 20),
        cost_estimate=pl.CostEstimate(
            flops=size * planes * rows * lanes,
            bytes_accessed=6 * size * planes * rows * lanes,
            transcendentals=0,
        ),
    )(cells, cells)


def filter_kernel(ends_ref, own_ref, low_ref, high_ref, diag_ref, out_ref, even, odd):
    total, rows, lanes = diag_ref.shape
    planes = total - 2 * HALO
    flat = own_ref.reshape(GROUP * planes * rows, lanes)
    lane = lax.broadcasted_iota(jnp.int32, (GROUP, lanes), 1)
    first, last = lane == 0, lane == lanes - 1

    def fill(p, carry):
        for y in range(rows):
            even[p, y] = low_ref[p, y].astype(f32)
            even[p + HALO + planes, y] = high_ref[p, y].astype(f32)
        return carry

    lax.fori_loop(0, HALO, fill, 0)

    def copy(p, carry):
        for y in range(rows):
            at = pl.ds(p * rows + y, GROUP, stride=planes * rows)
            even[p + HALO, y] = flat[at, :]
        return carry

    lax.fori_loop(0, planes, copy, 0)

    def step(source, target, weight, reach, scale):
        def plane(p, carry):
            below = None
            here = source[p, 0]
            for y in range(rows):
                above = source[p, y + 1] if y + 1 < rows else None
                left = jnp.where(first, 0.0, pltpu.roll(here, 1, 1))
                right = jnp.where(last, 0.0, pltpu.roll(here, lanes - 1, 1))
                beside = (source[p - 1, y] + source[p + 1, y]) + (left + right)
                if below is not None:
                    beside = beside + below
                if above is not None:
                    beside = beside + above
                value = diag_ref[p, pl.ds(y, 1), :] * here - beside
                if weight:
                    value = value - weight * target[p, y]
                if scale:
                    out_ref[y // 2, 2 * (p - HALO) + y % 2] = (value * scale).astype(bf16)
                else:
                    target[p, y] = value
                below, here = here, above
            return carry

        lax.fori_loop(reach, total - reach, plane, 0)
        if reach < HALO:
            zero = jnp.zeros((GROUP, lanes), f32)

            def clear(at):
                def one(p, carry):
                    for y in range(rows):
                        target[at + p, y] = zero
                    return carry

                lax.fori_loop(0, HALO - reach, one, 0)

            @pl.when(ends_ref[0] == 1)
            def _():
                clear(reach)

            @pl.when(ends_ref[1] == 1)
            def _():
                clear(HALO + planes)

    step(even, odd, 0.0, 1, 0.0)
    step(odd, even, 24.5, 2, 0.0)
    step(even, odd, 12.25, 3, 0.0)
    step(odd, even, 12.25, 4, 8.0 / 2401.0)


def filtered(ends, cells, low, high, diag, chunk, size):
    total, rows, lanes = diag.shape
    planes = total - 2 * HALO
    groups = size // GROUP
    edge = pl.BlockSpec((HALO, rows, GROUP, lanes), lambda g: (0, 0, g, 0))
    return pl.pallas_call(
        filter_kernel,
        out_shape=jax.ShapeDtypeStruct((rows // 2, 2 * planes, size, lanes), bf16),
        grid=(groups,),
        in_specs=[
            pl.BlockSpec(memory_space=pltpu.SMEM),
            pl.BlockSpec((GROUP, planes * rows, lanes), lambda g: (chunk * groups + g, 0, 0)),
            edge,
            edge,
            pl.BlockSpec((total, rows, lanes), lambda g: (0, 0, 0)),
        ],
        out_specs=pl.BlockSpec((rows // 2, 2 * planes, GROUP, lanes), lambda g: (0, 0, g, 0)),
        scratch_shapes=[pltpu.VMEM((total, rows, GROUP, lanes), f32)] * 2,
        compiler_params=pltpu.CompilerParams(vmem_limit_bytes=24 << 20),
        cost_estimate=pl.CostEstimate(
            flops=12 * 44 * rows * size * lanes, bytes_accessed=5 << 20, transcendentals=0
        ),
    )(ends, cells, low, high, diag)


def project_kernel(place_ref, ritz_ref, cells_ref, out_ref, *refs):
    *kept_refs, total = refs
    step = pl.program_id(0)
    lanes = cells_ref.shape[3]

    @pl.when(step == 0)
    def _():
        total[...] = jnp.zeros_like(total)

    part = jnp.concatenate(
        [cells_ref[:, k].reshape(-1, lanes) for k in range(STEP)], axis=1
    )
    total[...] += jnp.dot(
        part, ritz_ref[...].reshape(STEP * lanes, -1), preferred_element_type=f32
    )
    for kept_ref in kept_refs:
        kept_ref[pl.ds(STEP * step, STEP)] = ritz_ref[...]

    @pl.when(step == pl.num_programs(0) - 1)
    def _():
        near, size, _ = out_ref.shape
        if out_ref.dtype == f32:
            for q in range(near):
                out_ref[place_ref[0] ^ q] = total[q * size : (q + 1) * size, :]
        else:
            out_ref[...] = total[...].astype(bf16).reshape(out_ref.shape)


def projected(cells, ritz, near, place, kind):
    blocks, rows, vectors, lanes = cells.shape
    kept = ritz.shape[2]
    count = blocks * vectors
    out_shape = [jax.ShapeDtypeStruct((near, count // near, kept), kind)]
    out_specs = [pl.BlockSpec((near, count // near, kept), lambda r: (0, 0, 0))]
    if kind == bf16:
        out_shape.append(pltpu.VMEM(ritz.shape, ritz.dtype))
        out_specs.append(pl.BlockSpec(memory_space=pltpu.VMEM))
    return pl.pallas_call(
        project_kernel,
        out_shape=out_shape,
        grid=(rows // STEP,),
        in_specs=[
            pl.BlockSpec(memory_space=pltpu.SMEM),
            pl.BlockSpec((STEP, lanes, kept), lambda r: (r, 0, 0)),
            pl.BlockSpec((blocks, STEP, vectors, lanes), lambda r: (0, r, 0, 0)),
        ],
        out_specs=out_specs,
        scratch_shapes=[pltpu.VMEM((count, kept), f32)],
        compiler_params=pltpu.CompilerParams(vmem_limit_bytes=24 << 20),
        cost_estimate=pl.CostEstimate(
            flops=2 * count * rows * lanes * kept, bytes_accessed=7 << 20, transcendentals=0
        ),
    )(place, ritz, cells)


def remove_kernel(core_ref, mine_ref, other_ref, ritz_ref, *refs):
    out_ref = refs[-1]
    blocks, rows, vectors, lanes = refs[0].shape
    mine = mine_ref[...].reshape(blocks * vectors // 2, -1)
    other = other_ref[...].reshape(blocks * vectors // 2, -1)
    first = core_ref[0] == 0
    coeffs = jnp.concatenate(
        [jnp.where(first, mine, other), jnp.where(first, other, mine)], axis=0
    )

    def remove(cells_ref):
        for r in range(0, rows, 2):
            removed = lax.dot_general(
                coeffs,
                ritz_ref[r : r + 2].reshape(2 * lanes, -1),
                (((1,), (1,)), ((), ())),
                preferred_element_type=f32,
            )
            for k in range(2):
                for i in range(blocks):
                    held = cells_ref[i, r + k].astype(f32)
                    part = removed[i * vectors : (i + 1) * vectors, k * lanes : (k + 1) * lanes]
                    out_ref[i, pl.ds(r + k, vectors, stride=rows), :] = held - part

    for k, cells_ref in enumerate(refs[:-1]):
        pl.when(pl.program_id(0) == k)(functools.partial(remove, cells_ref))


def residual(core, mine, other, ritz, held):
    blocks, rows, vectors, lanes = held[0].shape
    near, _, kept = mine.shape
    chunks = len(held)
    size = mine.shape[1] // chunks
    coeffs = pl.BlockSpec((near, size, kept), lambda k: (0, k, 0))
    return pl.pallas_call(
        remove_kernel,
        out_shape=jax.ShapeDtypeStruct((blocks, chunks * vectors * rows, lanes), f32),
        grid=(chunks,),
        in_specs=[
            pl.BlockSpec(memory_space=pltpu.SMEM),
            coeffs,
            coeffs,
            pl.BlockSpec(memory_space=pltpu.VMEM),
            *([pl.BlockSpec((blocks, rows, vectors, lanes), lambda k: (0, 0, 0, 0))] * chunks),
        ],
        out_specs=pl.BlockSpec((blocks, vectors * rows, lanes), lambda k: (0, k, 0)),
        compiler_params=pltpu.CompilerParams(vmem_limit_bytes=32 << 20),
        cost_estimate=pl.CostEstimate(
            flops=2 * chunks * blocks * vectors * rows * lanes * kept,
            bytes_accessed=11 << 20,
            transcendentals=0,
        ),
    )(core, mine, other, ritz, *held)


def total_of(terms):
    while len(terms) > 1:
        terms = [a + b for a, b in zip(terms[::2], terms[1::2])]
    return terms[0]


def traded(blocks, axis):
    count = lax.axis_size(axis)
    return total_of(
        [blocks[0]]
        + [
            lax.ppermute(blocks[k], axis, [(i, i ^ k) for i in range(count)])
            for k in range(1, count)
        ]
    )


def near_sum(partial):
    if partial.dtype == bf16:
        blocks = lax.all_to_all(partial, NEAR, 0, 0, tiled=True)
        return jnp.sum(blocks.astype(f32), axis=0)
    for axis in NEAR:
        count = lax.axis_size(axis)
        partial = traded(partial.reshape(count, -1, *partial.shape[-2:]), axis)
    return partial[0]


def summed(parts):
    blocks = jnp.concatenate(parts, axis=0)
    blocks = blocks + swapped(blocks, "zh")
    blocks = traded([blocks] * lax.axis_size("zl"), "zl").astype(bf16)
    mine = from_everyone(blocks, SHARE)
    return mine, swapped(mine, "c")


def swapped(value, axis):
    return lax.ppermute(value, axis, [(0, 1), (1, 0)])


def from_everyone(value, axis):
    copies = jnp.broadcast_to(value, (lax.axis_size(axis), *value.shape))
    return lax.all_to_all(copies, axis, split_axis=0, concat_axis=0, tiled=True)


def swap_ends(low, high):
    count = lax.axis_size(DOM)
    from_below = lax.ppermute(high, DOM, [(i, i + 1) for i in range(count - 1)])
    from_above = lax.ppermute(low, DOM, [(i + 1, i) for i in range(count - 1)])
    return from_below, from_above


def pipeline(vectors, coefficient, ritz):
    count, planes, rows, lanes = vectors.shape
    size = count // CHUNKS
    other = swapped(coefficient, "zh")
    first = lax.axis_index("zh") == 0
    diag = jnp.stack(
        [jnp.where(first, coefficient, other), jnp.where(first, other, coefficient)]
    )
    diag = from_everyone(diag, ("x", "c"))
    diag = diag.transpose(2, 1, 0, 3, 4).reshape(planes, rows, lanes) + (6.0 - 7.125)
    below, above = swap_ends(diag[:HALO], diag[-HALO:])
    diag = jnp.concatenate([below, diag, above], axis=0)
    place = lax.axis_index(DOM)
    ends = jnp.stack([place == 0, place == lax.axis_size(DOM) - 1]).astype(jnp.int32)
    cells = pltpu.with_memory_space_constraint(
        vectors.reshape(count, planes * rows, lanes), pltpu.MemorySpace.HBM
    )
    ritz_rows = pltpu.with_memory_space_constraint(
        ritz.reshape(-1, *ritz.shape[2:]), pltpu.MemorySpace.HBM
    )
    held, parts = [], []
    for k in range(CHUNKS):
        low, high = spread(cells, rows, k, size)
        low, high = swap_ends(low, high)
        blocks = filtered(ends, cells, low, high, diag, k, size)
        held.append(lax.all_to_all(blocks, VEC, 0, 0, tiled=True))
    column = lax.axis_index(NEAR).reshape(1).astype(jnp.int32)
    for k in range(CHUNKS):
        kind = bf16 if k == CHUNKS - 1 else f32
        partial, *kept = projected(held[k], ritz_rows, lax.axis_size(NEAR), column, kind)
        if parts:
            partial, parts[-1] = lax.optimization_barrier((partial, parts[-1]))
        parts.append(near_sum(partial))
    mine, other = summed(parts)
    core = lax.axis_index("c").reshape(1).astype(jnp.int32)
    out = residual(core, mine, other, kept[0], held)
    return out.reshape(-1, *coefficient.shape)


def solution(mesh):
    fine = Mesh(mesh.devices.reshape(2, 4, 2, 4, 4), ("zh", "x", "c", "y", "zl"))
    placed = (P(VEC, DOM, None, None), P(DOM, VEC, None), P(DOM, VEC, None, None))
    return jax.shard_map(
        pipeline, mesh=fine, in_specs=placed, out_specs=P(None, DOM, VEC, None), check_vma=False
    )
```

```python
import functools

import jax
import jax.numpy as jnp
from jax import lax
from jax.experimental import pallas as pl
from jax.experimental.pallas import tpu as pltpu
from jax.sharding import Mesh, PartitionSpec as P

bf16 = jnp.bfloat16
f32 = jnp.float32

VEC = ("zh", "x", "c")
DOM = ("y", "zl")
SHARE = ("y", "x")
NEAR = ("c", *SHARE)
HALO = 4
GROUP = 16
CHUNKS = 2
STEP = 4


def spread_kernel(first_ref, second_ref, low_ref, high_ref):
    for source, target in ((first_ref, low_ref), (second_ref, high_ref)):
        planes, rows = target.shape[:2]
        vectors, span, lanes = source.shape
        flat = source.reshape(vectors * span, lanes)
        for p in range(planes):
            for y in range(rows):
                at = pl.ds(p * rows + y, vectors, stride=span)
                target[p, y] = flat[at, :].astype(bf16)


def spread(cells, rows, chunk, size):
    planes, lanes = cells.shape[1] // rows, cells.shape[2]
    half = planes // 2
    steps = half // 2
    out = pl.BlockSpec((2, rows, size, lanes), lambda p: (p, 0, 0, 0))
    return pl.pallas_call(
        spread_kernel,
        out_shape=[jax.ShapeDtypeStruct((half, rows, size, lanes), bf16)] * 2,
        grid=(steps,),
        in_specs=[
            pl.BlockSpec((size, 2 * rows, lanes), lambda p: (chunk, p, 0)),
            pl.BlockSpec((size, 2 * rows, lanes), lambda p: (chunk, p + steps, 0)),
        ],
        out_specs=[out] * 2,
        compiler_params=pltpu.CompilerParams(vmem_limit_bytes=10 << 20),
        cost_estimate=pl.CostEstimate(
            flops=size * planes * rows * lanes,
            bytes_accessed=6 * size * planes * rows * lanes,
            transcendentals=0,
        ),
    )(cells, cells)


def filter_kernel(ends_ref, own_ref, low_ref, high_ref, diag_ref, out_ref, even, odd):
    total, rows, lanes = diag_ref.shape
    planes = total - 2 * HALO
    flat = own_ref.reshape(GROUP * planes * rows, lanes)
    lane = lax.broadcasted_iota(jnp.int32, (GROUP, lanes), 1)
    first, last = lane == 0, lane == lanes - 1

    def fill(p, carry):
        for y in range(rows):
            even[p, y] = low_ref[p, y].astype(f32)
            even[p + HALO + planes, y] = high_ref[p, y].astype(f32)
        return carry

    lax.fori_loop(0, HALO, fill, 0)

    def copy(p, carry):
        for y in range(rows):
            at = pl.ds(p * rows + y, GROUP, stride=planes * rows)
            even[p + HALO, y] = flat[at, :]
        return carry

    lax.fori_loop(0, planes, copy, 0)

    def step(source, target, weight, reach, scale):
        def plane(p, carry):
            below = None
            here = source[p, 0]
            for y in range(rows):
                above = source[p, y + 1] if y + 1 < rows else None
                left = jnp.where(first, 0.0, pltpu.roll(here, 1, 1))
                right = jnp.where(last, 0.0, pltpu.roll(here, lanes - 1, 1))
                beside = (source[p - 1, y] + source[p + 1, y]) + (left + right)
                if below is not None:
                    beside = beside + below
                if above is not None:
                    beside = beside + above
                value = diag_ref[p, pl.ds(y, 1), :] * here - beside
                if weight:
                    value = value - weight * target[p, y]
                if scale:
                    out_ref[y // 2, 2 * (p - HALO) + y % 2] = (value * scale).astype(bf16)
                else:
                    target[p, y] = value
                below, here = here, above
            return carry

        lax.fori_loop(reach, total - reach, plane, 0)
        if reach < HALO:
            zero = jnp.zeros((GROUP, lanes), f32)

            def clear(at):
                def one(p, carry):
                    for y in range(rows):
                        target[at + p, y] = zero
                    return carry

                lax.fori_loop(0, HALO - reach, one, 0)

            @pl.when(ends_ref[0] == 1)
            def _():
                clear(reach)

            @pl.when(ends_ref[1] == 1)
            def _():
                clear(HALO + planes)

    step(even, odd, 0.0, 1, 0.0)
    step(odd, even, 24.5, 2, 0.0)
    step(even, odd, 12.25, 3, 0.0)
    step(odd, even, 12.25, 4, 8.0 / 2401.0)


def filtered(ends, cells, low, high, diag, chunk, size):
    total, rows, lanes = diag.shape
    planes = total - 2 * HALO
    groups = size // GROUP
    edge = pl.BlockSpec((HALO, rows, GROUP, lanes), lambda g: (0, 0, g, 0))
    return pl.pallas_call(
        filter_kernel,
        out_shape=jax.ShapeDtypeStruct((rows // 2, 2 * planes, size, lanes), bf16),
        grid=(groups,),
        in_specs=[
            pl.BlockSpec(memory_space=pltpu.SMEM),
            pl.BlockSpec((GROUP, planes * rows, lanes), lambda g: (chunk * groups + g, 0, 0)),
            edge,
            edge,
            pl.BlockSpec((total, rows, lanes), lambda g: (0, 0, 0)),
        ],
        out_specs=pl.BlockSpec((rows // 2, 2 * planes, GROUP, lanes), lambda g: (0, 0, g, 0)),
        scratch_shapes=[pltpu.VMEM((total, rows, GROUP, lanes), f32)] * 2,
        compiler_params=pltpu.CompilerParams(vmem_limit_bytes=24 << 20),
        cost_estimate=pl.CostEstimate(
            flops=12 * 44 * rows * size * lanes, bytes_accessed=5 << 20, transcendentals=0
        ),
    )(ends, cells, low, high, diag)


def project_kernel(place_ref, ritz_ref, cells_ref, out_ref, *refs):
    *kept_refs, total = refs
    step = pl.program_id(0)
    lanes = cells_ref.shape[3]

    @pl.when(step == 0)
    def _():
        total[...] = jnp.zeros_like(total)

    part = jnp.concatenate(
        [cells_ref[:, k].reshape(-1, lanes) for k in range(STEP)], axis=1
    )
    total[...] += jnp.dot(
        part, ritz_ref[...].reshape(STEP * lanes, -1), preferred_element_type=f32
    )
    for kept_ref in kept_refs:
        kept_ref[pl.ds(STEP * step, STEP)] = ritz_ref[...]

    @pl.when(step == pl.num_programs(0) - 1)
    def _():
        near, size, _ = out_ref.shape
        if out_ref.dtype == f32:
            for q in range(near):
                out_ref[place_ref[0] ^ q] = total[q * size : (q + 1) * size, :]
        else:
            out_ref[...] = total[...].astype(bf16).reshape(out_ref.shape)


def projected(cells, ritz, near, place, kind):
    blocks, rows, vectors, lanes = cells.shape
    kept = ritz.shape[2]
    count = blocks * vectors
    out_shape = [jax.ShapeDtypeStruct((near, count // near, kept), kind)]
    out_specs = [pl.BlockSpec((near, count // near, kept), lambda r: (0, 0, 0))]
    if kind == bf16:
        out_shape.append(pltpu.VMEM(ritz.shape, ritz.dtype))
        out_specs.append(pl.BlockSpec(memory_space=pltpu.VMEM))
    return pl.pallas_call(
        project_kernel,
        out_shape=out_shape,
        grid=(rows // STEP,),
        in_specs=[
            pl.BlockSpec(memory_space=pltpu.SMEM),
            pl.BlockSpec((STEP, lanes, kept), lambda r: (r, 0, 0)),
            pl.BlockSpec((blocks, STEP, vectors, lanes), lambda r: (0, r, 0, 0)),
        ],
        out_specs=out_specs,
        scratch_shapes=[pltpu.VMEM((count, kept), f32)],
        compiler_params=pltpu.CompilerParams(vmem_limit_bytes=24 << 20),
        cost_estimate=pl.CostEstimate(
            flops=2 * count * rows * lanes * kept, bytes_accessed=7 << 20, transcendentals=0
        ),
    )(place, ritz, cells)


def remove_kernel(core_ref, mine_ref, other_ref, ritz_ref, *refs):
    out_ref = refs[-1]
    blocks, rows, vectors, lanes = refs[0].shape
    mine = mine_ref[...].reshape(blocks * vectors // 2, -1)
    other = other_ref[...].reshape(blocks * vectors // 2, -1)
    first = core_ref[0] == 0
    coeffs = jnp.concatenate(
        [jnp.where(first, mine, other), jnp.where(first, other, mine)], axis=0
    )

    def remove(cells_ref):
        flat = out_ref.reshape(blocks * vectors * rows, lanes)
        for r in range(0, rows, STEP):
            removed = lax.dot_general(
                coeffs,
                ritz_ref[pl.ds(pl.program_id(1) * rows + r, STEP)].reshape(STEP * lanes, -1),
                (((1,), (1,)), ((), ())),
                preferred_element_type=f32,
            )
            for k in range(STEP):
                for i in range(blocks):
                    held = cells_ref[i, r + k].astype(f32)
                    part = removed[i * vectors : (i + 1) * vectors, k * lanes : (k + 1) * lanes]
                    at = pl.ds(i * vectors * rows + r + k, vectors, stride=rows)
                    flat[at, :] = held - part

    for k, cells_ref in enumerate(refs[:-1]):
        pl.when(pl.program_id(0) == k)(functools.partial(remove, cells_ref))


def residual(core, mine, other, ritz, held):
    blocks, rows, vectors, lanes = held[0].shape
    near, _, kept = mine.shape
    chunks = len(held)
    size = mine.shape[1] // chunks
    coeffs = pl.BlockSpec((near, size, kept), lambda k, g: (0, k, 0))
    part = rows // 2
    cells = pl.BlockSpec((blocks, part, vectors, lanes), lambda k, g: (0, g, 0, 0))
    return pl.pallas_call(
        remove_kernel,
        out_shape=jax.ShapeDtypeStruct((blocks, chunks * vectors, rows, lanes), f32),
        grid=(chunks, 2),
        in_specs=[
            pl.BlockSpec(memory_space=pltpu.SMEM),
            coeffs,
            coeffs,
            pl.BlockSpec(memory_space=pltpu.VMEM),
            *([cells] * chunks),
        ],
        out_specs=pl.BlockSpec((blocks, vectors, part, lanes), lambda k, g: (0, k, g, 0)),
        compiler_params=pltpu.CompilerParams(vmem_limit_bytes=24 << 20),
        cost_estimate=pl.CostEstimate(
            flops=2 * chunks * blocks * vectors * rows * lanes * kept,
            bytes_accessed=11 << 20,
            transcendentals=0,
        ),
    )(core, mine, other, ritz, *held)


def total_of(terms):
    while len(terms) > 1:
        terms = [a + b for a, b in zip(terms[::2], terms[1::2])]
    return terms[0]


def traded(blocks, axis):
    count = lax.axis_size(axis)
    return total_of(
        [blocks[0]]
        + [
            lax.ppermute(blocks[k], axis, [(i, i ^ k) for i in range(count)])
            for k in range(1, count)
        ]
    )


def near_sum(partial):
    if partial.dtype == bf16:
        blocks = lax.all_to_all(partial, NEAR, 0, 0, tiled=True)
        return jnp.sum(blocks.astype(f32), axis=0)
    for axis in NEAR:
        count = lax.axis_size(axis)
        partial = traded(partial.reshape(count, -1, *partial.shape[-2:]), axis)
    return partial[0]


def summed(parts):
    blocks = jnp.concatenate(parts, axis=0)
    blocks = blocks + swapped(blocks, "zh")
    blocks = traded([blocks] * lax.axis_size("zl"), "zl").astype(bf16)
    mine = from_everyone(blocks, SHARE)
    return mine, swapped(mine, "c")


def swapped(value, axis):
    return lax.ppermute(value, axis, [(0, 1), (1, 0)])


def from_everyone(value, axis):
    copies = jnp.broadcast_to(value, (lax.axis_size(axis), *value.shape))
    return lax.all_to_all(copies, axis, split_axis=0, concat_axis=0, tiled=True)


def swap_ends(low, high):
    count = lax.axis_size(DOM)
    from_below = lax.ppermute(high, DOM, [(i, i + 1) for i in range(count - 1)])
    from_above = lax.ppermute(low, DOM, [(i + 1, i) for i in range(count - 1)])
    return from_below, from_above


def pipeline(vectors, coefficient, ritz):
    count, planes, rows, lanes = vectors.shape
    size = count // CHUNKS
    other = swapped(coefficient, "zh")
    first = lax.axis_index("zh") == 0
    diag = jnp.stack(
        [jnp.where(first, coefficient, other), jnp.where(first, other, coefficient)]
    )
    diag = from_everyone(diag, ("x", "c"))
    diag = diag.transpose(2, 1, 0, 3, 4).reshape(planes, rows, lanes) + (6.0 - 7.125)
    below, above = swap_ends(diag[:HALO], diag[-HALO:])
    diag = jnp.concatenate([below, diag, above], axis=0)
    place = lax.axis_index(DOM)
    ends = jnp.stack([place == 0, place == lax.axis_size(DOM) - 1]).astype(jnp.int32)
    cells = pltpu.with_memory_space_constraint(
        vectors.reshape(count, planes * rows, lanes), pltpu.MemorySpace.HBM
    )
    ritz_rows = pltpu.with_memory_space_constraint(
        ritz.reshape(-1, *ritz.shape[2:]), pltpu.MemorySpace.HBM
    )
    held, parts = [], []
    for k in range(CHUNKS):
        low, high = spread(cells, rows, k, size)
        low, high = swap_ends(low, high)
        blocks = filtered(ends, cells, low, high, diag, k, size)
        held.append(lax.all_to_all(blocks, VEC, 0, 0, tiled=True))
    column = lax.axis_index(NEAR).reshape(1).astype(jnp.int32)
    for k in range(CHUNKS):
        kind = bf16 if k == CHUNKS - 1 else f32
        partial, *kept = projected(held[k], ritz_rows, lax.axis_size(NEAR), column, kind)
        if parts:
            partial, parts[-1] = lax.optimization_barrier((partial, parts[-1]))
        parts.append(near_sum(partial))
    mine, other = summed(parts)
    core = lax.axis_index("c").reshape(1).astype(jnp.int32)
    out = residual(core, mine, other, kept[0], held)
    return out.reshape(-1, *coefficient.shape)


def solution(mesh):
    fine = Mesh(mesh.devices.reshape(2, 4, 2, 4, 4), ("zh", "x", "c", "y", "zl"))
    placed = (P(VEC, DOM, None, None), P(DOM, VEC, None), P(DOM, VEC, None, None))
    return jax.shard_map(
        pipeline, mesh=fine, in_specs=placed, out_specs=P(None, DOM, VEC, None), check_vma=False
    )
```

```python
import jax
import jax.numpy as jnp
from jax import lax
from jax.experimental import pallas as pl
from jax.experimental.pallas import tpu as pltpu
from jax.sharding import Mesh, PartitionSpec as P

bf16 = jnp.bfloat16
f32 = jnp.float32

VEC = ("zh", "x", "c")
DOM = ("y", "zl")
SHARE = ("y", "x")
NEAR = ("c", *SHARE)
HALO = 4
GROUP = 16
CHUNKS = 2
STEP = 4


def spread_kernel(first_ref, second_ref, low_ref, high_ref):
    for source, target in ((first_ref, low_ref), (second_ref, high_ref)):
        planes, rows = target.shape[:2]
        vectors, span, lanes = source.shape
        flat = source.reshape(vectors * span, lanes)
        for p in range(planes):
            for y in range(rows):
                at = pl.ds(p * rows + y, vectors, stride=span)
                target[p, y] = flat[at, :].astype(bf16)


def spread(cells, rows, chunk, size):
    planes, lanes = cells.shape[1] // rows, cells.shape[2]
    half = planes // 2
    steps = half // 2
    out = pl.BlockSpec((2, rows, size, lanes), lambda p: (p, 0, 0, 0))
    return pl.pallas_call(
        spread_kernel,
        out_shape=[jax.ShapeDtypeStruct((half, rows, size, lanes), bf16)] * 2,
        grid=(steps,),
        in_specs=[
            pl.BlockSpec((size, 2 * rows, lanes), lambda p: (chunk, p, 0)),
            pl.BlockSpec((size, 2 * rows, lanes), lambda p: (chunk, p + steps, 0)),
        ],
        out_specs=[out] * 2,
        compiler_params=pltpu.CompilerParams(vmem_limit_bytes=10 << 20),
        cost_estimate=pl.CostEstimate(
            flops=size * planes * rows * lanes,
            bytes_accessed=6 * size * planes * rows * lanes,
            transcendentals=0,
        ),
    )(cells, cells)


def filter_kernel(ends_ref, own_ref, low_ref, high_ref, diag_ref, out_ref, even, odd):
    total, rows, lanes = diag_ref.shape
    planes = total - 2 * HALO
    flat = own_ref.reshape(GROUP * planes * rows, lanes)
    lane = lax.broadcasted_iota(jnp.int32, (GROUP, lanes), 1)
    first, last = lane == 0, lane == lanes - 1

    def fill(p, carry):
        for y in range(rows):
            even[p, y] = low_ref[p, y].astype(f32)
            even[p + HALO + planes, y] = high_ref[p, y].astype(f32)
        return carry

    lax.fori_loop(0, HALO, fill, 0)

    def copy(p, carry):
        for y in range(rows):
            at = pl.ds(p * rows + y, GROUP, stride=planes * rows)
            even[p + HALO, y] = flat[at, :]
        return carry

    lax.fori_loop(0, planes, copy, 0)

    def step(source, target, weight, reach, scale):
        def plane(p, carry):
            below = None
            here = source[p, 0]
            for y in range(rows):
                above = source[p, y + 1] if y + 1 < rows else None
                left = jnp.where(first, 0.0, pltpu.roll(here, 1, 1))
                right = jnp.where(last, 0.0, pltpu.roll(here, lanes - 1, 1))
                beside = (source[p - 1, y] + source[p + 1, y]) + (left + right)
                if below is not None:
                    beside = beside + below
                if above is not None:
                    beside = beside + above
                value = diag_ref[p, pl.ds(y, 1), :] * here - beside
                if weight:
                    value = value - weight * target[p, y]
                if scale:
                    out_ref[y // 2, 2 * (p - HALO) + y % 2] = (value * scale).astype(bf16)
                else:
                    target[p, y] = value
                below, here = here, above
            return carry

        lax.fori_loop(reach, total - reach, plane, 0)
        if reach < HALO:
            zero = jnp.zeros((GROUP, lanes), f32)

            def clear(at):
                def one(p, carry):
                    for y in range(rows):
                        target[at + p, y] = zero
                    return carry

                lax.fori_loop(0, HALO - reach, one, 0)

            @pl.when(ends_ref[0] == 1)
            def _():
                clear(reach)

            @pl.when(ends_ref[1] == 1)
            def _():
                clear(HALO + planes)

    step(even, odd, 0.0, 1, 0.0)
    step(odd, even, 24.5, 2, 0.0)
    step(even, odd, 12.25, 3, 0.0)
    step(odd, even, 12.25, 4, 8.0 / 2401.0)


def filtered(ends, cells, low, high, diag, chunk, size):
    total, rows, lanes = diag.shape
    planes = total - 2 * HALO
    groups = size // GROUP
    edge = pl.BlockSpec((HALO, rows, GROUP, lanes), lambda g: (0, 0, g, 0))
    return pl.pallas_call(
        filter_kernel,
        out_shape=jax.ShapeDtypeStruct((rows // 2, 2 * planes, size, lanes), bf16),
        grid=(groups,),
        in_specs=[
            pl.BlockSpec(memory_space=pltpu.SMEM),
            pl.BlockSpec((GROUP, planes * rows, lanes), lambda g: (chunk * groups + g, 0, 0)),
            edge,
            edge,
            pl.BlockSpec((total, rows, lanes), lambda g: (0, 0, 0)),
        ],
        out_specs=pl.BlockSpec((rows // 2, 2 * planes, GROUP, lanes), lambda g: (0, 0, g, 0)),
        scratch_shapes=[pltpu.VMEM((total, rows, GROUP, lanes), f32)] * 2,
        compiler_params=pltpu.CompilerParams(vmem_limit_bytes=24 << 20),
        cost_estimate=pl.CostEstimate(
            flops=12 * 44 * rows * size * lanes, bytes_accessed=5 << 20, transcendentals=0
        ),
    )(ends, cells, low, high, diag)


def project_kernel(place_ref, ritz_ref, cells_ref, out_ref, *refs):
    *kept_refs, total = refs
    step = pl.program_id(0)
    lanes = cells_ref.shape[3]

    @pl.when(step == 0)
    def _():
        total[...] = jnp.zeros_like(total)

    part = jnp.concatenate(
        [cells_ref[:, k].reshape(-1, lanes) for k in range(STEP)], axis=1
    )
    total[...] += jnp.dot(
        part, ritz_ref[...].reshape(STEP * lanes, -1), preferred_element_type=f32
    )
    for kept_ref in kept_refs:
        kept_ref[pl.ds(STEP * step, STEP)] = ritz_ref[...]

    @pl.when(step == pl.num_programs(0) - 1)
    def _():
        near, size, _ = out_ref.shape
        if out_ref.dtype == f32:
            for q in range(near):
                out_ref[place_ref[0] ^ q] = total[q * size : (q + 1) * size, :]
        else:
            out_ref[...] = total[...].astype(bf16).reshape(out_ref.shape)


def projected(cells, ritz, near, place, kind):
    blocks, rows, vectors, lanes = cells.shape
    kept = ritz.shape[2]
    count = blocks * vectors
    out_shape = [jax.ShapeDtypeStruct((near, count // near, kept), kind)]
    out_specs = [pl.BlockSpec((near, count // near, kept), lambda r: (0, 0, 0))]
    if kind == bf16:
        out_shape.append(pltpu.VMEM(ritz.shape, ritz.dtype))
        out_specs.append(pl.BlockSpec(memory_space=pltpu.VMEM))
    return pl.pallas_call(
        project_kernel,
        out_shape=out_shape,
        grid=(rows // STEP,),
        in_specs=[
            pl.BlockSpec(memory_space=pltpu.SMEM),
            pl.BlockSpec((STEP, lanes, kept), lambda r: (r, 0, 0)),
            pl.BlockSpec((blocks, STEP, vectors, lanes), lambda r: (0, r, 0, 0)),
        ],
        out_specs=out_specs,
        scratch_shapes=[pltpu.VMEM((count, kept), f32)],
        compiler_params=pltpu.CompilerParams(vmem_limit_bytes=24 << 20),
        cost_estimate=pl.CostEstimate(
            flops=2 * count * rows * lanes * kept, bytes_accessed=7 << 20, transcendentals=0
        ),
    )(place, ritz, cells)


def remove_kernel(half_ref, coeffs_ref, ritz_ref, *refs):
    out_ref, cells_refs = refs[-1], refs[:CHUNKS]
    blocks, rows, vectors, lanes = cells_refs[0].shape
    near, size, kept = coeffs_ref.shape
    size = size // CHUNKS
    coeffs = coeffs_ref[...].reshape(near * CHUNKS * size, kept)
    flat = out_ref.reshape(blocks * CHUNKS * vectors * rows, lanes)
    for r in range(0, rows, STEP):
        removed = lax.dot_general(
            coeffs,
            ritz_ref[pl.ds(pl.program_id(0) * rows + r, STEP)].reshape(STEP * lanes, -1),
            (((1,), (1,)), ((), ())),
            preferred_element_type=f32,
        )
        for j in range(near * CHUNKS):
            chunk, row = j % CHUNKS, j // CHUNKS * size
            block, vector = row // vectors, row % vectors
            for k in range(STEP):
                held = cells_refs[chunk][block, r + k, vector : vector + size].astype(f32)
                part = removed[j * size : (j + 1) * size, k * lanes : (k + 1) * lanes]
                place = (block * CHUNKS + chunk) * vectors + vector
                flat[pl.ds(place * rows + r + k, size, stride=rows), :] = held - part


def residual(half, coeffs, ritz, held, out):
    blocks, rows, vectors, lanes = held[0].shape
    blocks, part = blocks // 2, rows // 2
    cells = pl.BlockSpec((blocks, part, vectors, lanes), lambda g, half: (half[0], g, 0, 0))
    specs = [
        pl.BlockSpec(coeffs.shape, lambda g, half: (0, 0, 0)),
        pl.BlockSpec(memory_space=pltpu.VMEM),
        *([cells] * CHUNKS),
    ]
    operands = [half, coeffs, ritz, *held]
    if out is not None:
        specs.append(pl.BlockSpec(memory_space=pl.ANY))
        operands.append(out)
    count = CHUNKS * vectors
    return pl.pallas_call(
        remove_kernel,
        out_shape=jax.ShapeDtypeStruct((2 * blocks, count, rows, lanes), f32),
        grid_spec=pltpu.PrefetchScalarGridSpec(
            num_scalar_prefetch=1,
            grid=(2,),
            in_specs=specs,
            out_specs=pl.BlockSpec(
                (blocks, count, part, lanes), lambda g, half: (half[0], 0, g, 0)
            ),
        ),
        input_output_aliases={} if out is None else {len(operands) - 1: 0},
        compiler_params=pltpu.CompilerParams(vmem_limit_bytes=24 << 20),
        cost_estimate=pl.CostEstimate(
            flops=2 * count * blocks * rows * lanes * ritz.shape[2],
            bytes_accessed=4 << 20,
            transcendentals=0,
        ),
    )(*operands)


def total_of(terms):
    while len(terms) > 1:
        terms = [a + b for a, b in zip(terms[::2], terms[1::2])]
    return terms[0]


def traded(blocks, axis):
    count = lax.axis_size(axis)
    return total_of(
        [blocks[0]]
        + [
            lax.ppermute(blocks[k], axis, [(i, i ^ k) for i in range(count)])
            for k in range(1, count)
        ]
    )


def near_sum(partial):
    if partial.dtype == bf16:
        blocks = lax.all_to_all(partial, NEAR, 0, 0, tiled=True)
        return jnp.sum(blocks.astype(f32), axis=0)
    for axis in NEAR:
        count = lax.axis_size(axis)
        partial = traded(partial.reshape(count, -1, *partial.shape[-2:]), axis)
    return partial[0]


def summed(parts):
    blocks = jnp.concatenate(parts, axis=0)
    blocks = blocks + swapped(blocks, "zh")
    blocks = traded([blocks] * lax.axis_size("zl"), "zl").astype(bf16)
    mine = from_everyone(blocks, SHARE)
    return mine, swapped(mine, "c")


def swapped(value, axis):
    return lax.ppermute(value, axis, [(0, 1), (1, 0)])


def from_everyone(value, axis):
    copies = jnp.broadcast_to(value, (lax.axis_size(axis), *value.shape))
    return lax.all_to_all(copies, axis, split_axis=0, concat_axis=0, tiled=True)


def swap_ends(low, high):
    count = lax.axis_size(DOM)
    from_below = lax.ppermute(high, DOM, [(i, i + 1) for i in range(count - 1)])
    from_above = lax.ppermute(low, DOM, [(i + 1, i) for i in range(count - 1)])
    return from_below, from_above


def pipeline(vectors, coefficient, ritz):
    count, planes, rows, lanes = vectors.shape
    size = count // CHUNKS
    other = swapped(coefficient, "zh")
    first = lax.axis_index("zh") == 0
    diag = jnp.stack(
        [jnp.where(first, coefficient, other), jnp.where(first, other, coefficient)]
    )
    diag = from_everyone(diag, ("x", "c"))
    diag = diag.transpose(2, 1, 0, 3, 4).reshape(planes, rows, lanes) + (6.0 - 7.125)
    below, above = swap_ends(diag[:HALO], diag[-HALO:])
    diag = jnp.concatenate([below, diag, above], axis=0)
    place = lax.axis_index(DOM)
    ends = jnp.stack([place == 0, place == lax.axis_size(DOM) - 1]).astype(jnp.int32)
    cells = pltpu.with_memory_space_constraint(
        vectors.reshape(count, planes * rows, lanes), pltpu.MemorySpace.HBM
    )
    ritz_rows = pltpu.with_memory_space_constraint(
        ritz.reshape(-1, *ritz.shape[2:]), pltpu.MemorySpace.HBM
    )
    held, parts = [], []
    for k in range(CHUNKS):
        low, high = spread(cells, rows, k, size)
        low, high = swap_ends(low, high)
        blocks = filtered(ends, cells, low, high, diag, k, size)
        held.append(lax.all_to_all(blocks, VEC, 0, 0, tiled=True))
    column = lax.axis_index(NEAR).reshape(1).astype(jnp.int32)
    for k in range(CHUNKS):
        kind = bf16 if k == CHUNKS - 1 else f32
        partial, *kept = projected(held[k], ritz_rows, lax.axis_size(NEAR), column, kind)
        if parts:
            partial, parts[-1] = lax.optimization_barrier((partial, parts[-1]))
        parts.append(near_sum(partial))
    mine, other = summed(parts)
    core = lax.axis_index("c").reshape(1).astype(jnp.int32)
    out = residual(core, mine, kept[0], held, None)
    out = residual(1 - core, other, kept[0], held, out)
    return out.reshape(-1, *coefficient.shape)


def solution(mesh):
    fine = Mesh(mesh.devices.reshape(2, 4, 2, 4, 4), ("zh", "x", "c", "y", "zl"))
    placed = (P(VEC, DOM, None, None), P(DOM, VEC, None), P(DOM, VEC, None, None))
    return jax.shard_map(
        pipeline, mesh=fine, in_specs=placed, out_specs=P(None, DOM, VEC, None), check_vma=False
    )
```

```python
import jax
import jax.numpy as jnp
from jax import lax
from jax.experimental import pallas as pl
from jax.experimental.pallas import tpu as pltpu
from jax.sharding import Mesh, PartitionSpec as P

bf16 = jnp.bfloat16
f32 = jnp.float32

VEC = ("zh", "x", "c")
DOM = ("y", "zl")
SHARE = ("y", "x")
NEAR = ("c", *SHARE)
HALO = 4
GROUP = 16
CHUNKS = 2
STEP = 4
WIDE = 8


def spread_kernel(first_ref, second_ref, low_ref, high_ref):
    for source, target in ((first_ref, low_ref), (second_ref, high_ref)):
        planes, rows = target.shape[:2]
        vectors, span, lanes = source.shape
        flat = source.reshape(vectors * span, lanes)
        for p in range(planes):
            for y in range(rows):
                at = pl.ds(p * rows + y, vectors, stride=span)
                target[p, y] = flat[at, :].astype(bf16)


def spread(cells, rows, chunk, size):
    planes, lanes = cells.shape[1] // rows, cells.shape[2]
    half = planes // 2
    steps = half // 2
    out = pl.BlockSpec((2, rows, size, lanes), lambda p: (p, 0, 0, 0))
    return pl.pallas_call(
        spread_kernel,
        out_shape=[jax.ShapeDtypeStruct((half, rows, size, lanes), bf16)] * 2,
        grid=(steps,),
        in_specs=[
            pl.BlockSpec((size, 2 * rows, lanes), lambda p: (chunk, p, 0)),
            pl.BlockSpec((size, 2 * rows, lanes), lambda p: (chunk, p + steps, 0)),
        ],
        out_specs=[out] * 2,
        compiler_params=pltpu.CompilerParams(vmem_limit_bytes=10 << 20),
        cost_estimate=pl.CostEstimate(
            flops=size * planes * rows * lanes,
            bytes_accessed=6 * size * planes * rows * lanes,
            transcendentals=0,
        ),
    )(cells, cells)


def filter_kernel(ends_ref, own_ref, low_ref, high_ref, diag_ref, out_ref, even, odd):
    total, rows, lanes = diag_ref.shape
    planes = total - 2 * HALO
    flat = own_ref.reshape(GROUP * planes * rows, lanes)
    lane = lax.broadcasted_iota(jnp.int32, (GROUP, lanes), 1)
    first, last = lane == 0, lane == lanes - 1

    def fill(p, carry):
        for y in range(rows):
            even[p, y] = low_ref[p, y].astype(f32)
            even[p + HALO + planes, y] = high_ref[p, y].astype(f32)
        return carry

    lax.fori_loop(0, HALO, fill, 0)

    def copy(p, carry):
        for y in range(rows):
            at = pl.ds(p * rows + y, GROUP, stride=planes * rows)
            even[p + HALO, y] = flat[at, :]
        return carry

    lax.fori_loop(0, planes, copy, 0)

    def step(source, target, weight, reach, scale):
        def plane(p, carry):
            below = None
            here = source[p, 0]
            for y in range(rows):
                above = source[p, y + 1] if y + 1 < rows else None
                left = jnp.where(first, 0.0, pltpu.roll(here, 1, 1))
                right = jnp.where(last, 0.0, pltpu.roll(here, lanes - 1, 1))
                beside = (source[p - 1, y] + source[p + 1, y]) + (left + right)
                if below is not None:
                    beside = beside + below
                if above is not None:
                    beside = beside + above
                value = diag_ref[p, pl.ds(y, 1), :] * here - beside
                if weight:
                    value = value - weight * target[p, y]
                if scale:
                    out_ref[y // 2, 2 * (p - HALO) + y % 2] = (value * scale).astype(bf16)
                else:
                    target[p, y] = value
                below, here = here, above
            return carry

        lax.fori_loop(reach, total - reach, plane, 0)
        if reach < HALO:
            zero = jnp.zeros((GROUP, lanes), f32)

            def clear(at):
                def one(p, carry):
                    for y in range(rows):
                        target[at + p, y] = zero
                    return carry

                lax.fori_loop(0, HALO - reach, one, 0)

            @pl.when(ends_ref[0] == 1)
            def _():
                clear(reach)

            @pl.when(ends_ref[1] == 1)
            def _():
                clear(HALO + planes)

    step(even, odd, 0.0, 1, 0.0)
    step(odd, even, 24.5, 2, 0.0)
    step(even, odd, 12.25, 3, 0.0)
    step(odd, even, 12.25, 4, 8.0 / 2401.0)


def filtered(ends, cells, low, high, diag, chunk, size):
    total, rows, lanes = diag.shape
    planes = total - 2 * HALO
    groups = size // GROUP
    edge = pl.BlockSpec((HALO, rows, GROUP, lanes), lambda g: (0, 0, g, 0))
    return pl.pallas_call(
        filter_kernel,
        out_shape=jax.ShapeDtypeStruct((rows // 2, 2 * planes, size, lanes), bf16),
        grid=(groups,),
        in_specs=[
            pl.BlockSpec(memory_space=pltpu.SMEM),
            pl.BlockSpec((GROUP, planes * rows, lanes), lambda g: (chunk * groups + g, 0, 0)),
            edge,
            edge,
            pl.BlockSpec((total, rows, lanes), lambda g: (0, 0, 0)),
        ],
        out_specs=pl.BlockSpec((rows // 2, 2 * planes, GROUP, lanes), lambda g: (0, 0, g, 0)),
        scratch_shapes=[pltpu.VMEM((total, rows, GROUP, lanes), f32)] * 2,
        compiler_params=pltpu.CompilerParams(vmem_limit_bytes=24 << 20),
        cost_estimate=pl.CostEstimate(
            flops=12 * 44 * rows * size * lanes, bytes_accessed=5 << 20, transcendentals=0
        ),
    )(ends, cells, low, high, diag)


def project_kernel(place_ref, ritz_ref, cells_ref, out_ref, *refs):
    *kept_refs, total = refs
    step = pl.program_id(0)
    lanes = cells_ref.shape[3]

    @pl.when(step == 0)
    def _():
        total[...] = jnp.zeros_like(total)

    part = jnp.concatenate(
        [cells_ref[:, k].reshape(-1, lanes) for k in range(WIDE)], axis=1
    )
    total[...] += jnp.dot(
        part, ritz_ref[...].reshape(WIDE * lanes, -1), preferred_element_type=f32
    )
    for kept_ref in kept_refs:
        kept_ref[pl.ds(WIDE * step, WIDE)] = ritz_ref[...]

    @pl.when(step == pl.num_programs(0) - 1)
    def _():
        near, size, _ = out_ref.shape
        if out_ref.dtype == f32:
            for q in range(near):
                out_ref[place_ref[0] ^ q] = total[q * size : (q + 1) * size, :]
        else:
            out_ref[...] = total[...].astype(bf16).reshape(out_ref.shape)


def projected(cells, ritz, near, place, kind):
    blocks, rows, vectors, lanes = cells.shape
    kept = ritz.shape[2]
    count = blocks * vectors
    out_shape = [jax.ShapeDtypeStruct((near, count // near, kept), kind)]
    out_specs = [pl.BlockSpec((near, count // near, kept), lambda r: (0, 0, 0))]
    if kind == bf16:
        out_shape.append(pltpu.VMEM(ritz.shape, ritz.dtype))
        out_specs.append(pl.BlockSpec(memory_space=pltpu.VMEM))
    return pl.pallas_call(
        project_kernel,
        out_shape=out_shape,
        grid=(rows // WIDE,),
        in_specs=[
            pl.BlockSpec(memory_space=pltpu.SMEM),
            pl.BlockSpec((WIDE, lanes, kept), lambda r: (r, 0, 0)),
            pl.BlockSpec((blocks, WIDE, vectors, lanes), lambda r: (0, r, 0, 0)),
        ],
        out_specs=out_specs,
        scratch_shapes=[pltpu.VMEM((count, kept), f32)],
        compiler_params=pltpu.CompilerParams(vmem_limit_bytes=24 << 20),
        cost_estimate=pl.CostEstimate(
            flops=2 * count * rows * lanes * kept, bytes_accessed=7 << 20, transcendentals=0
        ),
    )(place, ritz, cells)


def remove_kernel(half_ref, coeffs_ref, ritz_ref, *refs):
    out_ref, cells_refs = refs[-1], refs[:CHUNKS]
    blocks, rows, vectors, lanes = cells_refs[0].shape
    near, size, kept = coeffs_ref.shape
    size = size // CHUNKS
    coeffs = coeffs_ref[...].reshape(near * CHUNKS * size, kept)
    flat = out_ref.reshape(blocks * CHUNKS * vectors * rows, lanes)
    for r in range(0, rows, STEP):
        removed = lax.dot_general(
            coeffs,
            ritz_ref[pl.ds(pl.program_id(0) * rows + r, STEP)].reshape(STEP * lanes, -1),
            (((1,), (1,)), ((), ())),
            preferred_element_type=f32,
        )
        for j in range(near * CHUNKS):
            chunk, row = j % CHUNKS, j // CHUNKS * size
            block, vector = row // vectors, row % vectors
            for k in range(STEP):
                held = cells_refs[chunk][block, r + k, vector : vector + size].astype(f32)
                part = removed[j * size : (j + 1) * size, k * lanes : (k + 1) * lanes]
                place = (block * CHUNKS + chunk) * vectors + vector
                flat[pl.ds(place * rows + r + k, size, stride=rows), :] = held - part


def residual(half, coeffs, ritz, held, out):
    blocks, rows, vectors, lanes = held[0].shape
    blocks, part = blocks // 2, rows // 2
    cells = pl.BlockSpec((blocks, part, vectors, lanes), lambda g, half: (half[0], g, 0, 0))
    specs = [
        pl.BlockSpec(coeffs.shape, lambda g, half: (0, 0, 0)),
        pl.BlockSpec(memory_space=pltpu.VMEM),
        *([cells] * CHUNKS),
    ]
    operands = [half, coeffs, ritz, *held]
    if out is not None:
        specs.append(pl.BlockSpec(memory_space=pl.ANY))
        operands.append(out)
    count = CHUNKS * vectors
    return pl.pallas_call(
        remove_kernel,
        out_shape=jax.ShapeDtypeStruct((2 * blocks, count, rows, lanes), f32),
        grid_spec=pltpu.PrefetchScalarGridSpec(
            num_scalar_prefetch=1,
            grid=(2,),
            in_specs=specs,
            out_specs=pl.BlockSpec(
                (blocks, count, part, lanes), lambda g, half: (half[0], 0, g, 0)
            ),
        ),
        input_output_aliases={} if out is None else {len(operands) - 1: 0},
        compiler_params=pltpu.CompilerParams(vmem_limit_bytes=24 << 20),
        cost_estimate=pl.CostEstimate(
            flops=2 * count * blocks * rows * lanes * ritz.shape[2],
            bytes_accessed=4 << 20,
            transcendentals=0,
        ),
    )(*operands)


def total_of(terms):
    while len(terms) > 1:
        terms = [a + b for a, b in zip(terms[::2], terms[1::2])]
    return terms[0]


def traded(blocks, axis):
    count = lax.axis_size(axis)
    return total_of(
        [blocks[0]]
        + [
            lax.ppermute(blocks[k], axis, [(i, i ^ k) for i in range(count)])
            for k in range(1, count)
        ]
    )


def near_sum(partial):
    if partial.dtype == bf16:
        blocks = lax.all_to_all(partial, NEAR, 0, 0, tiled=True)
        return jnp.sum(blocks.astype(f32), axis=0)
    for axis in NEAR:
        count = lax.axis_size(axis)
        partial = traded(partial.reshape(count, -1, *partial.shape[-2:]), axis)
    return partial[0]


def summed(parts):
    blocks = jnp.concatenate(parts, axis=0)
    blocks = blocks + swapped(blocks, "zh")
    blocks = traded([blocks] * lax.axis_size("zl"), "zl").astype(bf16)
    mine = from_everyone(blocks, SHARE)
    return mine, swapped(mine, "c")


def swapped(value, axis):
    return lax.ppermute(value, axis, [(0, 1), (1, 0)])


def from_everyone(value, axis):
    copies = jnp.broadcast_to(value, (lax.axis_size(axis), *value.shape))
    return lax.all_to_all(copies, axis, split_axis=0, concat_axis=0, tiled=True)


def swap_ends(low, high):
    count = lax.axis_size(DOM)
    from_below = lax.ppermute(high, DOM, [(i, i + 1) for i in range(count - 1)])
    from_above = lax.ppermute(low, DOM, [(i + 1, i) for i in range(count - 1)])
    return from_below, from_above


def pipeline(vectors, coefficient, ritz):
    count, planes, rows, lanes = vectors.shape
    size = count // CHUNKS
    other = swapped(coefficient, "zh")
    first = lax.axis_index("zh") == 0
    diag = jnp.stack(
        [jnp.where(first, coefficient, other), jnp.where(first, other, coefficient)]
    )
    diag = from_everyone(diag, ("x", "c"))
    diag = diag.transpose(2, 1, 0, 3, 4).reshape(planes, rows, lanes) + (6.0 - 7.125)
    below, above = swap_ends(diag[:HALO], diag[-HALO:])
    diag = jnp.concatenate([below, diag, above], axis=0)
    place = lax.axis_index(DOM)
    ends = jnp.stack([place == 0, place == lax.axis_size(DOM) - 1]).astype(jnp.int32)
    cells = pltpu.with_memory_space_constraint(
        vectors.reshape(count, planes * rows, lanes), pltpu.MemorySpace.HBM
    )
    ritz_rows = pltpu.with_memory_space_constraint(
        ritz.reshape(-1, *ritz.shape[2:]), pltpu.MemorySpace.HBM
    )
    held, parts = [], []
    for k in range(CHUNKS):
        low, high = spread(cells, rows, k, size)
        low, high = swap_ends(low, high)
        blocks = filtered(ends, cells, low, high, diag, k, size)
        held.append(lax.all_to_all(blocks, VEC, 0, 0, tiled=True))
    column = lax.axis_index(NEAR).reshape(1).astype(jnp.int32)
    for k in range(CHUNKS):
        kind = bf16 if k == CHUNKS - 1 else f32
        partial, *kept = projected(held[k], ritz_rows, lax.axis_size(NEAR), column, kind)
        if parts:
            partial, parts[-1] = lax.optimization_barrier((partial, parts[-1]))
        parts.append(near_sum(partial))
    mine, other = summed(parts)
    core = lax.axis_index("c").reshape(1).astype(jnp.int32)
    out = residual(core, mine, kept[0], held, None)
    out = residual(1 - core, other, kept[0], held, out)
    return out.reshape(-1, *coefficient.shape)


def solution(mesh):
    fine = Mesh(mesh.devices.reshape(2, 4, 2, 4, 4), ("zh", "x", "c", "y", "zl"))
    placed = (P(VEC, DOM, None, None), P(DOM, VEC, None), P(DOM, VEC, None, None))
    return jax.shard_map(
        pipeline, mesh=fine, in_specs=placed, out_specs=P(None, DOM, VEC, None), check_vma=False
    )
```
